32 devices in a mesh: grp: 4 (over y, x), slab: 8 (over z, core).
Axes of the slice: x: 2, y: 2, z: 4, core: 2. Of those that a mesh axis runs over, the one named last changes fastest.
Arguments:
- templates: float32 [4, 8, 512, 512], P('grp', None, 'slab'), may hold values from -6 to 6
- momentum: float32 [4, 8, 512, 512], P('grp', None, 'slab'), may hold values from -6 to 6
- subjects: float32 [4, 8, 512, 512], P('grp', None, 'slab'), may hold values from -6 to 6
- smooth_x: float32 [512, 512], replicated, may hold values from 0 to 1
- smooth_y: float32 [512, 512], replicated, may hold values from 0 to 1
- smooth_z: float32 [8, 8], replicated, may hold values from 0 to 1.5
- owned_block: int32 [4], replicated, may hold values from 0 to 3, each once
Outputs:
- final_image: float32 [4, 8, 512, 512], P('grp', None, 'slab')
- final_momentum: float32 [4, 8, 512, 512], P('grp', None, 'slab')
- center_owned: float32 [4, 2, 512, 512], P('grp', None, 'slab')
- new_templates: float32 [4, 8, 512, 512], P('grp', None, 'slab')
The draws below stay inside these ranges and needn't reach their ends.
Inputs may be any that keep to these rules, and one draw needn't show every extreme that they name: `owned_block`: a permutation: every block has exactly one owning group.
All inputs are finite; a program needn't handle non-finite values.
Results may differ from the reference program's by a relative error of at most 0.0001.
Values sent between devices are 32-bit elements; how exact they have to be, the bound alone decides.
A program may use at most 64 MiB of HBM per device.

```python
import math
import jax
import jax.numpy as jnp
from jax import lax

N = 512
BLK_PLANES = 2
STEPS = 2
GROUPS = 4
PLANES = 8
ELL = 64
ELL_Z = 1


def kernel_matrix(key, order, length):
    index = jnp.arange(order)
    distance = jnp.abs(index[:, None] - index[None, :]).astype(jnp.float32)
    factor = jax.random.uniform(key, (order, order), jnp.float32, 0.5, 1.5)
    return jnp.exp(-distance / length) * factor / math.sqrt(length)


def draw_smooth_x(key, part):
    return kernel_matrix(jax.random.fold_in(key, 11), N, ELL)


def draw_smooth_y(key, part):
    return kernel_matrix(jax.random.fold_in(key, 23), N, ELL)


def draw_smooth_z(key, part):
    return kernel_matrix(jax.random.fold_in(key, 37), PLANES, ELL_Z)


def steps_of(own_key, shape, split, smallest, high):
    def one(dim, parts):
        steps = jax.random.uniform(jax.random.fold_in(jax.random.fold_in(own_key, 6), dim), (parts,), jnp.float32, smallest / len(split), high / len(split))
        return jnp.repeat(jnp.exp(steps), shape[dim] // parts).reshape((-1,) + (1,) * (len(shape) - dim - 1))

    level = one(*split[0])
    for cut in split[1:]:
        level = level * one(*cut)
    return level


def scatter_about(rng, dims, width, limit, split=(), held_as=jnp.bfloat16):
    entries = jax.random.normal(rng, dims, jnp.float32) * width
    if len(split) > 0:
        entries = steps_of(rng, dims, split, -0.22, 0.18) * entries
    return jnp.clip(entries, min=-limit, max=limit).astype(held_as)


def setup_inputs(seed: int = 0) -> dict:
    seeds = jax.random.split(jax.random.key(seed), 8)
    templates = scatter_about(seeds[0], (GROUPS, PLANES, N, N), 1.0, 6.0, ((0, 4), (2, 8)), jnp.float32)
    momentum = scatter_about(seeds[1], (GROUPS, PLANES, N, N), 1.0, 6.0, ((0, 4), (2, 8)), jnp.float32)
    subjects = scatter_about(seeds[2], (GROUPS, PLANES, N, N), 1.0, 6.0, ((0, 4), (2, 8)), jnp.float32)
    smooth_x = draw_smooth_x(jax.random.fold_in(seeds[7], 71), 0)
    smooth_y = draw_smooth_y(jax.random.fold_in(seeds[7], 71), 0)
    smooth_z = draw_smooth_z(jax.random.fold_in(seeds[7], 71), 0)
    owned_block = jax.random.permutation(seeds[6], GROUPS).astype(jnp.int32)
    return dict(templates=templates, momentum=momentum, subjects=subjects, smooth_x=smooth_x, smooth_y=smooth_y, smooth_z=smooth_z, owned_block=owned_block)


learn_rate = 0.5
pull_weight = 0.5


def diff_cols(field):
    zeros = jnp.zeros_like(field[..., :1])
    padded = jnp.concatenate([zeros, field, zeros], axis=-1)
    return (padded[..., 2:] - padded[..., :-2]) * 0.5


def diff_rows(field):
    zeros = jnp.zeros_like(field[..., :1, :])
    padded = jnp.concatenate([zeros, field, zeros], axis=-2)
    return (padded[..., 2:, :] - padded[..., :-2, :]) * 0.5


def diff_planes(field):
    zeros = jnp.zeros_like(field[..., :1, :, :])
    padded = jnp.concatenate([zeros, field, zeros], axis=-3)
    return (padded[..., 2:, :, :] - padded[..., :-2, :, :]) * 0.5


def smooth(field, smooth_x, smooth_y, smooth_z):
    across = jnp.einsum('ij,gjyx->giyx', smooth_z, field, precision=lax.Precision.HIGHEST)
    along = jnp.einsum('ij,gpyj->gpyi', smooth_x, across, precision=lax.Precision.HIGHEST)
    return jnp.einsum('ij,gpjx->gpix', smooth_y, along, precision=lax.Precision.HIGHEST)


def reference(templates, momentum, subjects, smooth_x, smooth_y, smooth_z, owned_block):
    time_step = 1.0 / STEPS
    image = templates
    moment = momentum
    for section in range(STEPS):
        grad_cols = diff_cols(image)
        grad_rows = diff_rows(image)
        grad_planes = diff_planes(image)
        vel_cols = -smooth(moment * grad_cols, smooth_x, smooth_y, smooth_z)
        vel_rows = -smooth(moment * grad_rows, smooth_x, smooth_y, smooth_z)
        vel_planes = -smooth(moment * grad_planes, smooth_x, smooth_y, smooth_z)
        new_image = image - time_step * (vel_cols * grad_cols + vel_rows * grad_rows + vel_planes * grad_planes)
        new_moment = moment - time_step * (diff_cols(moment * vel_cols) + diff_rows(moment * vel_rows) + diff_planes(moment * vel_planes))
        image = new_image
        moment = new_moment
    update = templates - learn_rate * (image - subjects)
    center = jnp.sum(update, axis=0) / GROUPS
    blocks = center.reshape(GROUPS, BLK_PLANES, N, N)
    center_owned = jnp.take(blocks, owned_block.astype(jnp.int32), axis=0)
    new_templates = update + pull_weight * (center[None] - update)
    return image, moment, center_owned, new_templates
```

```python
import functools

import jax
import jax.numpy as jnp
from jax import lax
from jax.experimental import pallas as pl
from jax.experimental.pallas import tpu as pltpu
from jax.sharding import PartitionSpec as P

STEPS = 2
GATHER_BYTES = 16 * 2**20
EDGE = 8
PAD = 2 * EDGE
TILE = 16
RING = 4
VMEM_LIMIT = 60 * 2**20
MESH_ID = pl.DeviceIdType.MESH


learn_rate = 0.5
pull_weight = 0.5


def with_halo(cells, sides, width):
    for axis, dim in sides:
        count = lax.axis_size(axis)
        ends = count - 1
        head = lax.slice_in_dim(cells, 0, width, axis=dim)
        tail = lax.slice_in_dim(cells, cells.shape[dim] - width, cells.shape[dim], axis=dim)
        cells = jnp.concatenate(
            [
                lax.ppermute(tail, axis, [(i, (i + 1) % count) for i in range(ends)]),
                cells,
                lax.ppermute(head, axis, [((i + 1) % count, i) for i in range(ends)]),
            ],
            axis=dim,
        )
    return cells


def diff_cols(field):
    zeros = jnp.zeros_like(field[..., :1])
    padded = jnp.concatenate([zeros, field, zeros], axis=-1)
    return (padded[..., 2:] - padded[..., :-2]) * 0.5


def diff_planes(field):
    zeros = jnp.zeros_like(field[..., :1, :, :])
    padded = jnp.concatenate([zeros, field, zeros], axis=-3)
    return (padded[..., 2:, :, :] - padded[..., :-2, :, :]) * 0.5


def smooth_planes(field, smooth_z):
    return jnp.einsum("ij,cjyx->ciyx", smooth_z, field, precision=lax.Precision.HIGHEST)


def smooth_plane(field, smooth_x, smooth_y):
    along = jnp.einsum("ij,cpyj->cpyi", smooth_x, field, precision=lax.Precision.HIGHEST)
    return jnp.einsum("ij,cpjx->cpix", smooth_y, along, precision=lax.Precision.HIGHEST)


def diff_rows(field):
    zeros = jnp.zeros_like(field[..., :1, :])
    padded = jnp.concatenate([zeros, field, zeros], axis=-2)
    return (padded[..., 2:, :] - padded[..., :-2, :]) * 0.5


def rows_of(field, start, count):
    return lax.dynamic_slice_in_dim(field, start, count, field.ndim - 2)


def halve(field):
    high = field.astype(jnp.bfloat16)
    return high, (field - high.astype(jnp.float32)).astype(jnp.bfloat16)


def dot_pair(left, right):
    mul = lambda a, b: jnp.dot(a, b, preferred_element_type=jnp.float32)
    return mul(left[0], right[0]) + (mul(left[0], right[1]) + mul(left[1], right[0]))


def aligned(start, size, step=8):
    return pl.ds(pl.multiple_of(start, step), size)


def across(wide):
    return wide[EDGE + 1 : EDGE + 1 + TILE] - wide[EDGE - 1 : EDGE - 1 + TILE]


def whole_kernel(
    dims, smooth_z, owned_block, templates, momentum, subjects, smooth_x, smooth_y,
    image_out, moment_out, owned_out, template_out,
    raw, vel, moved, high, low, along, parts, swapped, first_in, second_in,
    padded_y, ext_high, ext_low, cols_high, cols_low, win_high, win_low,
    local_sems, up_sems, down_sems, side_sems, recv_sems,
    part_send, part_recv, pull_send, pull_recv,
):
    planes, rows, cols, own, chips = dims
    span = own + PAD
    pair = 2 * own
    half = rows // 2
    wide = pair + PAD
    me = lax.axis_index("slab")
    grp = lax.axis_index("grp")
    chip, core = me // 2, me % 2
    other = 1 - core
    sibling = chip * 2 + other
    scale = 0.5 / STEPS

    def own_rows(buffer_kind):
        return raw.at[buffer_kind, :, aligned(PAD + me * own, own), :]

    loads = [
        pltpu.make_async_copy(templates.at[0], own_rows(0), local_sems.at[0]),
        pltpu.make_async_copy(momentum.at[0], own_rows(1), local_sems.at[1]),
    ]
    mats = [
        pltpu.make_async_copy(smooth_y, padded_y.at[pl.ds(EDGE, rows), :], local_sems.at[2]),
        pltpu.make_async_copy(
            smooth_x.at[pl.ds(0, half), :], moved.at[0, pl.ds(0, half), :], local_sems.at[3]
        ),
        pltpu.make_async_copy(
            smooth_x.at[pl.ds(half, half), :], moved.at[1, pl.ds(0, half), :], local_sems.at[4]
        ),
    ]
    for copy in loads + mats:
        copy.start()

    barrier = pltpu.get_barrier_semaphore()

    def greet(where):
        pl.semaphore_signal(barrier, inc=1, device_id=where, device_id_type=MESH_ID)

    has_up, has_down = chip < chips - 1, chip > 0

    @pl.when(has_up)
    def _():
        greet({"slab": me + 2})

    @pl.when(has_down)
    def _():
        greet({"slab": me - 2})

    greet({"slab": sibling})
    across_x = jnp.where(grp % 2 == 0, grp + 1, grp - 1)
    across_y = (grp + 2) % 4
    greet({"grp": across_x})
    greet({"grp": across_y})
    pl.semaphore_wait(barrier, 3 + has_up.astype(jnp.int32) + has_down.astype(jnp.int32))

    for copy in loads:
        copy.wait()

    def send(plane, source, sem, target):
        piece = raw.at[:, plane, aligned(PAD + source * own, own), :]
        return pltpu.make_async_remote_copy(
            src_ref=piece, dst_ref=piece, send_sem=sem, recv_sem=recv_sems.at[plane, source],
            device_id={"slab": target}, device_id_type=MESH_ID,
        )

    def up(plane, distance):
        return send(plane, me - 2 * distance, up_sems.at[plane, distance], me + 2)

    def down(plane, distance):
        return send(plane, me + 2 * distance, down_sems.at[plane, distance], me - 2)

    def side(plane, which):
        return send(plane, which * 2 + core, side_sems.at[plane, which], sibling)

    def arrived(plane, source):
        send(plane, source, side_sems.at[plane, 0], sibling).wait_recv()

    def send_own(plane):
        @pl.when(has_up)
        def _():
            up(plane, 0).start()

        @pl.when(has_down)
        def _():
            down(plane, 0).start()

        side(plane, chip).start()

    ahead = min(2, planes)
    for plane in range(ahead):
        send_own(plane)

    zeros_pad = jnp.zeros((PAD, cols), jnp.float32)
    for kind in range(2):
        for plane in range(planes):
            raw[kind, plane, pl.ds(0, PAD), :] = zeros_pad
            raw[kind, plane, pl.ds(PAD + rows, PAD), :] = zeros_pad
    zeros_edge = jnp.zeros((EDGE, cols), jnp.float32)
    padded_y[pl.ds(0, EDGE), :] = zeros_edge
    padded_y[pl.ds(EDGE + rows, EDGE), :] = zeros_edge
    total = chips * span
    lines = total + PAD

    @pl.loop(0, 3 * planes)
    def _(at):
        @pl.loop(0, lines // TILE)
        def _(t):
            vel[at // planes, at % planes, aligned(t * TILE, TILE), :] = zeros_pad

    for copy in mats:
        copy.wait()
    turned = jnp.concatenate(
        [moved[0, pl.ds(0, half), :].T, moved[1, pl.ds(0, half), :].T], axis=1
    )
    cols_high[...], cols_low[...] = halve(turned)
    for b in range(chips):
        piece = padded_y[aligned(b * pair + core * own, span), :]
        ext_high[pl.ds(b * span, span), :], ext_low[pl.ds(b * span, span), :] = halve(piece)
    window = padded_y[aligned(chip * pair, wide), :]
    window = jnp.concatenate(
        [
            jnp.where(core == 0, window[:, b * pair : b * pair + own],
                      window[:, b * pair + own : (b + 1) * pair])
            for b in range(chips)
        ],
        axis=1,
    )
    win_high[...], win_low[...] = halve(window)

    column = lax.broadcasted_iota(jnp.int32, (TILE, cols), 1)
    is_first, is_last = column == 0, column == cols - 1

    def along_cols(tile):
        after = jnp.where(is_last, 0.0, pltpu.roll(tile, cols - 1, 1))
        return after - jnp.where(is_first, 0.0, pltpu.roll(tile, 1, 1))

    def keep(where, field, value):
        top = value.astype(jnp.bfloat16)
        high[field, where, :] = top
        low[field, where, :] = (value - top.astype(jnp.float32)).astype(jnp.bfloat16)

    def smooth(field, weights):
        along[...] = dot_pair((ext_high[...], ext_low[...]), (high[field], low[field]))
        along[...] = dot_pair(halve(along[...]), (cols_high[...], cols_low[...]))

        @pl.loop(0, total // TILE)
        def _(t):
            tile = along[aligned(t * TILE, TILE), :]
            into = aligned(EDGE + t * TILE, TILE)
            for i in range(planes):
                vel[field, i, into, :] += weights[i] * tile

    def plane_weights(plane):
        return [-0.5 * smooth_z[i, plane] for i in range(planes)]

    @pl.loop(0, planes)
    def _(plane):
        @pl.when(plane + ahead < planes)
        def _():
            send_own(plane + ahead)

        for distance in range(1, chips):

            @pl.when(chip >= distance)
            def _(distance=distance):
                arrived(plane, me - 2 * distance)
                if distance < chips - 1:

                    @pl.when(has_up)
                    def _():
                        up(plane, distance).start()

                side(plane, chip - distance).start()

            @pl.when(chip + distance < chips)
            def _(distance=distance):
                arrived(plane, me + 2 * distance)
                if distance < chips - 1:

                    @pl.when(has_down)
                    def _():
                        down(plane, distance).start()

                side(plane, chip + distance).start()

        for which in range(chips):
            arrived(plane, which * 2 + other)

        before = jnp.maximum(plane - 1, 0)
        far = jnp.maximum(plane - 2, 0)

        @pl.loop(0, rows // TILE)
        def _(t):
            here = aligned(PAD + t * TILE, TILE)
            into = aligned(t * TILE, TILE, TILE)
            wide_tile = raw[0, plane, aligned(EDGE + t * TILE, TILE + PAD), :]
            image, moment = wide_tile[EDGE : EDGE + TILE], raw[1, plane, here, :]
            keep(into, 0, moment * along_cols(image))
            keep(into, 1, moment * across(wide_tile))
            under = jnp.where(plane >= 2, raw[0, far, here, :], 0.0)
            keep(into, 2, raw[1, before, here, :] * (image - under))

        smooth(0, plane_weights(plane))
        smooth(1, plane_weights(plane))
        smooth(2, [jnp.where(plane >= 1, w, 0.0) for w in plane_weights(before)])

    last = planes - 1

    @pl.loop(0, rows // TILE)
    def _(t):
        here = aligned(PAD + t * TILE, TILE)
        keep(aligned(t * TILE, TILE, TILE), 2, raw[1, last, here, :] * (0.0 - raw[0, last - 1, here, :]))

    smooth(2, plane_weights(last))

    def part_copy(plane):
        return pltpu.make_async_remote_copy(
            src_ref=parts.at[plane % RING, :, aligned(other * own, span), :],
            dst_ref=swapped.at[plane],
            send_sem=part_send.at[plane], recv_sem=part_recv.at[plane],
            device_id={"slab": sibling}, device_id_type=MESH_ID,
        )

    @pl.loop(0, planes + 3)
    def _(turn):
        @pl.when(turn < planes)
        def _():
            plane = turn
            above, below = jnp.minimum(plane + 1, last), jnp.maximum(plane - 1, 0)

            @pl.loop(0, total // TILE)
            def _(t):
                b, k = t // (span // TILE), t % (span // TILE)
                g = b * pair + core * own + k * TILE + EDGE
                here, around = aligned(g, TILE), aligned(g - EDGE, TILE + PAD)
                at, at_around = aligned(t * TILE + EDGE, TILE), aligned(t * TILE, TILE + PAD)
                image_wide, moment_wide = raw[0, plane, around, :], raw[1, plane, around, :]
                image = image_wide[EDGE : EDGE + TILE]
                moment = moment_wide[EDGE : EDGE + TILE]
                row_wide = vel[1, plane, at_around, :]
                vel_c, vel_r = vel[0, plane, at, :], row_wide[EDGE : EDGE + TILE]
                vel_p = vel[2, plane, at, :]
                over = jnp.where(plane == last, 0.0, raw[0, above, here, :])
                under = jnp.where(plane == 0, 0.0, raw[0, below, here, :])
                push = (
                    vel_c * along_cols(image) + vel_r * across(image_wide) + vel_p * (over - under)
                )
                over = jnp.where(plane == last, 0.0, raw[1, above, here, :] * vel[2, above, at, :])
                under = jnp.where(plane == 0, 0.0, raw[1, below, here, :] * vel[2, below, at, :])
                flux = (
                    along_cols(moment * vel_c) + across(moment_wide * row_wide) + (over - under)
                )
                vel[0, plane, at, :] = image - scale * push
                moved[plane, aligned(t * TILE, TILE), :] = moment - scale * flux

        @pl.when((turn >= 1) & (turn <= planes))
        def _():
            plane = turn - 1
            above, below = jnp.minimum(plane + 1, last), jnp.maximum(plane - 1, 0)

            @pl.loop(0, half // TILE)
            def _(t):
                b, k = t // (own // TILE), t % (own // TILE)
                e = b * span + k * TILE + PAD
                at = aligned(e, TILE)
                into = aligned(t * TILE, TILE, TILE)
                image_wide = vel[0, plane, aligned(e - EDGE, TILE + PAD), :]
                image = image_wide[EDGE : EDGE + TILE]
                moment = moved[plane, aligned(e - EDGE, TILE), :]
                over = jnp.where(plane == last, 0.0, vel[0, above, at, :])
                under = jnp.where(plane == 0, 0.0, vel[0, below, at, :])
                keep(into, 0, moment * along_cols(image))
                keep(into, 1, moment * across(image_wide))
                keep(into, 2, moment * (over - under))

            @pl.when(plane >= RING)
            def _():
                part_copy(plane - RING).wait_send()

            inner = pl.ds(0, half)
            for field in range(3):
                parts[plane % RING, field] = dot_pair(
                    (win_high[...], win_low[...]), (high[field, inner, :], low[field, inner, :])
                )
            part_copy(plane).start()

        @pl.when(turn >= 3)
        def _():
            plane = turn - 3
            part_copy(plane).wait_recv()
            mine = aligned(core * own, span)
            both = parts[plane % RING, :, mine, :] + swapped[plane]
            out = dot_pair(halve(both.reshape(3 * span, cols)), (cols_high[...], cols_low[...]))
            swapped[plane] = out.reshape(3, span, cols)

    for plane in range(max(planes - RING, 0), planes):
        part_copy(plane).wait_send()

    subject_load = pltpu.make_async_copy(
        subjects.at[0], vel.at[2, :, pl.ds(own, own), :], local_sems.at[0]
    )
    subject_load.start()

    @pl.loop(0, 3 * (span // 8))
    def _(t):
        field, where = t // (span // 8), aligned((t % (span // 8)) * 8, 8)
        held = [swapped[j, field, where, :] for j in range(planes)]
        for i in range(planes):
            swapped[i, field, where, :] = -0.5 * sum(smooth_z[i, j] * held[j] for j in range(planes))

    subject_load.wait()

    image_at, moment_at, update_at = pl.ds(0, own), pl.ds(own, own), pl.ds(2 * own, own)
    sum_at, new_at = pl.ds(3 * own, own), pl.ds(4 * own, own)
    center_at, owned_at = pl.ds(0, own), pl.ds(2 * own, own)

    def pull_copy(plane, phase):
        source = vel.at[1, plane, update_at if phase == 0 else sum_at, :]
        by_x = plane % 2 == phase
        return pltpu.make_async_remote_copy(
            src_ref=source, dst_ref=(first_in, second_in)[phase].at[plane],
            send_sem=pull_send.at[phase, plane], recv_sem=pull_recv.at[phase, plane],
            device_id={"grp": jnp.where(by_x, across_x, across_y)}, device_id_type=MESH_ID,
        )

    @pl.loop(0, planes)
    def _(plane):
        above, below = jnp.minimum(plane + 1, last), jnp.maximum(plane - 1, 0)

        @pl.loop(0, own // TILE)
        def _(t):
            k = t * TILE
            e = chip * span + k + PAD
            at, around = aligned(e, TILE), aligned(e - EDGE, TILE + PAD)
            m_at, m_around = aligned(e - EDGE, TILE), aligned(e - PAD, TILE + PAD)
            v_at, v_around = aligned(k + EDGE, TILE), aligned(k, TILE + PAD)
            image_wide, moment_wide = vel[0, plane, around, :], moved[plane, m_around, :]
            image = image_wide[EDGE : EDGE + TILE]
            moment = moment_wide[EDGE : EDGE + TILE]
            row_wide = swapped[plane, 1, v_around, :]
            vel_c, vel_r = swapped[plane, 0, v_at, :], row_wide[EDGE : EDGE + TILE]
            vel_p = swapped[plane, 2, v_at, :]
            over = jnp.where(plane == last, 0.0, vel[0, above, at, :])
            under = jnp.where(plane == 0, 0.0, vel[0, below, at, :])
            push = vel_c * along_cols(image) + vel_r * across(image_wide) + vel_p * (over - under)
            over = jnp.where(
                plane == last, 0.0, moved[above, m_at, :] * swapped[above, 2, v_at, :]
            )
            under = jnp.where(plane == 0, 0.0, moved[below, m_at, :] * swapped[below, 2, v_at, :])
            flux = along_cols(moment * vel_c) + across(moment_wide * row_wide) + (over - under)
            new_image = image - scale * push
            vel[1, plane, aligned(k, TILE), :] = new_image
            vel[1, plane, aligned(own + k, TILE), :] = moment - scale * flux
            template = raw[0, plane, aligned(PAD + me * own + k, TILE), :]
            subject = vel[2, plane, aligned(own + k, TILE), :]
            vel[1, plane, aligned(2 * own + k, TILE), :] = template - learn_rate * (
                new_image - subject
            )

        pull_copy(plane, 0).start()

    stores = [
        pltpu.make_async_copy(vel.at[1, :, image_at, :], image_out.at[0], local_sems.at[1]),
        pltpu.make_async_copy(vel.at[1, :, moment_at, :], moment_out.at[0], local_sems.at[2]),
    ]
    for copy in stores:
        copy.start()

    @pl.loop(0, planes)
    def _(plane):
        pull_copy(plane, 0).wait_recv()
        vel[1, plane, sum_at, :] = vel[1, plane, update_at, :] + first_in[plane]
        pull_copy(plane, 1).start()

    @pl.loop(0, planes)
    def _(plane):
        pull_copy(plane, 1).wait_recv()
        center = (vel[1, plane, sum_at, :] + second_in[plane]) * 0.25
        update = vel[1, plane, update_at, :]
        vel[2, plane, center_at, :] = center
        vel[1, plane, new_at, :] = update + pull_weight * (center - update)

    stores.append(
        pltpu.make_async_copy(vel.at[1, :, new_at, :], template_out.at[0], local_sems.at[3])
    )
    stores[-1].start()
    block_planes = planes // 4
    mine = owned_block[grp]
    for k in range(block_planes):
        vel[2, k, owned_at, :] = vel[2, mine * block_planes + k, center_at, :]
    stores.append(
        pltpu.make_async_copy(
            vel.at[2, pl.ds(0, block_planes), owned_at, :], owned_out.at[0], local_sems.at[4]
        )
    )
    stores[-1].start()

    @pl.loop(0, planes)
    def _(plane):
        for distance in range(chips - 1):

            @pl.when(has_up & (chip >= distance))
            def _(distance=distance):
                up(plane, distance).wait_send()

            @pl.when(has_down & (chip + distance < chips))
            def _(distance=distance):
                down(plane, distance).wait_send()

        for which in range(chips):
            side(plane, which).wait_send()
        pull_copy(plane, 0).wait_send()
        pull_copy(plane, 1).wait_send()

    for copy in stores:
        copy.wait()


def on_device_whole(templates, momentum, subjects, smooth_x, smooth_y, smooth_z, owned_block):
    planes, own, cols = templates.shape[1:]
    rows = smooth_y.shape[0]
    chips = lax.axis_size("slab") // 2
    span, total = own + PAD, chips * (own + PAD)
    dims = (planes, rows, cols, own, chips)
    volume = jax.ShapeDtypeStruct(templates.shape, jnp.float32)
    owned = jax.ShapeDtypeStruct((1, planes // 4, own, cols), jnp.float32)
    any_space = pl.BlockSpec(memory_space=pl.ANY)
    smem = pl.BlockSpec(memory_space=pltpu.SMEM)
    f32 = lambda *shape: pltpu.VMEM(shape, jnp.float32)
    b16 = lambda *shape: pltpu.VMEM(shape, jnp.bfloat16)
    dma = lambda *shape: pltpu.SemaphoreType.DMA(shape)
    return pl.pallas_call(
        functools.partial(whole_kernel, dims),
        out_shape=(volume, volume, owned, volume),
        in_specs=[smem] * 2 + [any_space] * 5,
        out_specs=(any_space,) * 4,
        scratch_shapes=[
            f32(2, planes, rows + 2 * PAD, cols),
            f32(3, planes, total + PAD, cols),
            f32(planes, total, cols),
            b16(3, rows, cols),
            b16(3, rows, cols),
            f32(total, cols),
            f32(RING, 3, 2 * own + PAD, cols),
            f32(planes, 3, span, cols),
            f32(planes, own, cols),
            f32(planes, own, cols),
            f32(rows + PAD, cols),
            b16(total, rows),
            b16(total, rows),
            b16(cols, cols),
            b16(cols, cols),
            b16(2 * own + PAD, rows // 2),
            b16(2 * own + PAD, rows // 2),
            dma(5),
            dma(planes, chips - 1),
            dma(planes, chips - 1),
            dma(planes, chips),
            dma(planes, 2 * chips),
            dma(planes),
            dma(planes),
            dma(2, planes),
            dma(2, planes),
        ],
        compiler_params=pltpu.CompilerParams(
            collective_id=0, has_side_effects=True, vmem_limit_bytes=VMEM_LIMIT
        ),
        cost_estimate=pl.CostEstimate(
            flops=36 * planes * rows * rows * cols, bytes_accessed=2**24, transcendentals=0
        ),
    )(smooth_z, owned_block, templates, momentum, subjects, smooth_x, smooth_y)


def on_device(templates, momentum, subjects, smooth_x, smooth_y, smooth_z, owned_block):
    time_step = 1.0 / STEPS
    image = templates[0]
    moment = momentum[0]
    for section in range(STEPS):
        image_rows = with_halo(image, (("slab", 1),), 1)
        grad_rows = (image_rows[:, 2:, :] - image_rows[:, :-2, :]) * 0.5
        grad_cols = diff_cols(image)
        grad_planes = diff_planes(image)
        pushing = smooth_planes(
            jnp.stack([moment * grad_cols, moment * grad_rows, moment * grad_planes]), smooth_z
        )
        plane_fields = lax.all_to_all(pushing, "slab", split_axis=1, concat_axis=2, tiled=True)
        plane_vel = -smooth_plane(plane_fields, smooth_x, smooth_y)
        velocity = lax.all_to_all(plane_vel, "slab", split_axis=2, concat_axis=1, tiled=True)
        flux_edge = with_halo(moment * velocity[1], (("slab", 1),), 1)
        flux_rows = (flux_edge[:, 2:, :] - flux_edge[:, :-2, :]) * 0.5
        new_image = image - time_step * (
            velocity[0] * grad_cols + velocity[1] * grad_rows + velocity[2] * grad_planes
        )
        new_moment = moment - time_step * (
            diff_cols(moment * velocity[0]) + flux_rows + diff_planes(moment * velocity[2])
        )
        image = new_image
        moment = new_moment
    return finish(image, moment, templates, subjects, owned_block)


def finish(image, moment, templates, subjects, owned_block):
    update = templates[0] - learn_rate * (image - subjects[0])
    return (image[None], moment[None]) + pull(update, owned_block)


def sum_groups(field, orders):
    groups = lax.axis_size("grp")
    share = field.shape[0] // len(orders)
    pieces = [field[at * share : (at + 1) * share] for at in range(len(orders))]
    for turn in range(len(orders[0])):
        sent = [
            lax.ppermute(piece, "grp", [(i, i ^ order[turn]) for i in range(groups)])
            for piece, order in zip(pieces, orders)
        ]
        pieces = [piece + got for piece, got in zip(pieces, sent)]
    return jnp.concatenate(pieces, axis=0)


def pull(update, owned_block):
    groups = lax.axis_size("grp")
    planes_all = update.shape[0]
    block_planes = planes_all // groups
    if groups == 4 and planes_all % 2 == 0:
        center = sum_groups(update, ((1, 2), (2, 1))) / groups
    else:
        center = lax.psum(update, "grp") / groups
    owned_index = owned_block[lax.axis_index("grp")]
    owned_out = lax.dynamic_slice_in_dim(center, owned_index * block_planes, block_planes, 0)[None]
    new_template = update + pull_weight * (center - update)
    return (owned_out, new_template[None])


def solution(mesh):
    def body(*args):
        templates, smooth_y = args[0], args[4]
        gathered = 2 * 4 * templates.shape[1] * templates.shape[3] * smooth_y.shape[0]
        fits = gathered <= GATHER_BYTES and mesh.shape["grp"] == 4 and mesh.shape["slab"] % 2 == 0
        return (on_device_whole if fits else on_device)(*args)

    return jax.shard_map(
        body,
        mesh=mesh,
        in_specs=(
            P("grp", None, "slab", None),
            P("grp", None, "slab", None),
            P("grp", None, "slab", None),
            P(),
            P(),
            P(),
            P(),
        ),
        out_specs=(
            P("grp", None, "slab", None),
            P("grp", None, "slab", None),
            P("grp", None, "slab", None),
            P("grp", None, "slab", None),
        ),
        check_vma=False,
    )
```

```python
import functools

import jax
import jax.numpy as jnp
from jax import lax
from jax.experimental import pallas as pl
from jax.experimental.pallas import tpu as pltpu
from jax.sharding import PartitionSpec as P

STEPS = 2
GATHER_BYTES = 16 * 2**20
EDGE = 8
PAD = 2 * EDGE
TILE = 16
RING = 4
AHEAD = 8
LAG = 2
VMEM_LIMIT = 60 * 2**20
MESH_ID = pl.DeviceIdType.MESH


learn_rate = 0.5
pull_weight = 0.5


def with_halo(cells, sides, width):
    for axis, dim in sides:
        count = lax.axis_size(axis)
        ends = count - 1
        head = lax.slice_in_dim(cells, 0, width, axis=dim)
        tail = lax.slice_in_dim(cells, cells.shape[dim] - width, cells.shape[dim], axis=dim)
        cells = jnp.concatenate(
            [
                lax.ppermute(tail, axis, [(i, (i + 1) % count) for i in range(ends)]),
                cells,
                lax.ppermute(head, axis, [((i + 1) % count, i) for i in range(ends)]),
            ],
            axis=dim,
        )
    return cells


def diff_cols(field):
    zeros = jnp.zeros_like(field[..., :1])
    padded = jnp.concatenate([zeros, field, zeros], axis=-1)
    return (padded[..., 2:] - padded[..., :-2]) * 0.5


def diff_planes(field):
    zeros = jnp.zeros_like(field[..., :1, :, :])
    padded = jnp.concatenate([zeros, field, zeros], axis=-3)
    return (padded[..., 2:, :, :] - padded[..., :-2, :, :]) * 0.5


def smooth_planes(field, smooth_z):
    return jnp.einsum("ij,cjyx->ciyx", smooth_z, field, precision=lax.Precision.HIGHEST)


def smooth_plane(field, smooth_x, smooth_y):
    along = jnp.einsum("ij,cpyj->cpyi", smooth_x, field, precision=lax.Precision.HIGHEST)
    return jnp.einsum("ij,cpjx->cpix", smooth_y, along, precision=lax.Precision.HIGHEST)


def diff_rows(field):
    zeros = jnp.zeros_like(field[..., :1, :])
    padded = jnp.concatenate([zeros, field, zeros], axis=-2)
    return (padded[..., 2:, :] - padded[..., :-2, :]) * 0.5


def rows_of(field, start, count):
    return lax.dynamic_slice_in_dim(field, start, count, field.ndim - 2)


def halve(field):
    high = field.astype(jnp.bfloat16)
    return high, (field - high.astype(jnp.float32)).astype(jnp.bfloat16)


def dot_pair(left, right):
    mul = lambda a, b: jnp.dot(a, b, preferred_element_type=jnp.float32)
    return mul(left[0], right[0]) + (mul(left[0], right[1]) + mul(left[1], right[0]))


def aligned(start, size, step=8):
    return pl.ds(pl.multiple_of(start, step), size)


def across(wide):
    return wide[EDGE + 1 : EDGE + 1 + TILE] - wide[EDGE - 1 : EDGE - 1 + TILE]


def whole_kernel(
    dims, smooth_z, owned_block, templates, momentum, subjects, smooth_x, smooth_y,
    image_out, moment_out, owned_out, template_out,
    raw, vel, moved, high, low, along, parts, swapped, first_in, second_in,
    padded_y, ext_high, ext_low, cols_high, cols_low, win_high, win_low,
    local_sems, up_sems, down_sems, side_sems, recv_sems,
    part_send, part_recv, pull_send, pull_recv,
):
    planes, rows, cols, own, chips = dims
    span = own + PAD
    pair = 2 * own
    half = rows // 2
    wide = pair + PAD
    me = lax.axis_index("slab")
    grp = lax.axis_index("grp")
    chip, core = me // 2, me % 2
    other = 1 - core
    sibling = chip * 2 + other
    scale = 0.5 / STEPS

    def own_rows(buffer_kind):
        return raw.at[buffer_kind, :, aligned(PAD + me * own, own), :]

    loads = [
        pltpu.make_async_copy(templates.at[0], own_rows(0), local_sems.at[0]),
        pltpu.make_async_copy(momentum.at[0], own_rows(1), local_sems.at[1]),
    ]
    mats = [
        pltpu.make_async_copy(smooth_y, padded_y.at[pl.ds(EDGE, rows), :], local_sems.at[2]),
        pltpu.make_async_copy(
            smooth_x.at[pl.ds(0, half), :], moved.at[0, pl.ds(0, half), :], local_sems.at[3]
        ),
        pltpu.make_async_copy(
            smooth_x.at[pl.ds(half, half), :], moved.at[1, pl.ds(0, half), :], local_sems.at[4]
        ),
    ]
    for copy in loads + mats:
        copy.start()

    barrier = pltpu.get_barrier_semaphore()

    def greet(where):
        pl.semaphore_signal(barrier, inc=1, device_id=where, device_id_type=MESH_ID)

    has_up, has_down = chip < chips - 1, chip > 0

    @pl.when(has_up)
    def _():
        greet({"slab": me + 2})

    @pl.when(has_down)
    def _():
        greet({"slab": me - 2})

    greet({"slab": sibling})
    across_x = jnp.where(grp % 2 == 0, grp + 1, grp - 1)
    across_y = (grp + 2) % 4
    greet({"grp": across_x})
    greet({"grp": across_y})
    pl.semaphore_wait(barrier, 3 + has_up.astype(jnp.int32) + has_down.astype(jnp.int32))

    for copy in loads:
        copy.wait()

    def send(plane, source, sem, target):
        piece = raw.at[:, plane, aligned(PAD + source * own, own), :]
        return pltpu.make_async_remote_copy(
            src_ref=piece, dst_ref=piece, send_sem=sem, recv_sem=recv_sems.at[plane, source],
            device_id={"slab": target}, device_id_type=MESH_ID,
        )

    def up(plane, distance):
        return send(plane, me - 2 * distance, up_sems.at[plane, distance], me + 2)

    def down(plane, distance):
        return send(plane, me + 2 * distance, down_sems.at[plane, distance], me - 2)

    def side(plane, which):
        return send(plane, which * 2 + core, side_sems.at[plane, which], sibling)

    def arrived(plane, source):
        send(plane, source, side_sems.at[plane, 0], sibling).wait_recv()

    def send_own(plane):
        @pl.when(has_up)
        def _():
            up(plane, 0).start()

        @pl.when(has_down)
        def _():
            down(plane, 0).start()

        side(plane, chip).start()

    ahead = min(AHEAD, planes)
    for plane in range(ahead):
        send_own(plane)

    zeros_pad = jnp.zeros((PAD, cols), jnp.float32)
    for kind in range(2):
        for plane in range(planes):
            raw[kind, plane, pl.ds(0, PAD), :] = zeros_pad
            raw[kind, plane, pl.ds(PAD + rows, PAD), :] = zeros_pad
    zeros_edge = jnp.zeros((EDGE, cols), jnp.float32)
    padded_y[pl.ds(0, EDGE), :] = zeros_edge
    padded_y[pl.ds(EDGE + rows, EDGE), :] = zeros_edge
    total = chips * span
    lines = total + PAD

    @pl.loop(0, 3 * planes)
    def _(at):
        @pl.loop(0, lines // TILE, unroll=3)
        def _(t):
            vel[at // planes, at % planes, aligned(t * TILE, TILE), :] = zeros_pad

    for copy in mats:
        copy.wait()
    turned = jnp.concatenate(
        [moved[0, pl.ds(0, half), :].T, moved[1, pl.ds(0, half), :].T], axis=1
    )
    cols_high[...], cols_low[...] = halve(turned)
    for b in range(chips):
        piece = padded_y[aligned(b * pair + core * own, span), :]
        ext_high[pl.ds(b * span, span), :], ext_low[pl.ds(b * span, span), :] = halve(piece)
    window = padded_y[aligned(chip * pair, wide), :]
    window = jnp.concatenate(
        [
            jnp.where(core == 0, window[:, b * pair : b * pair + own],
                      window[:, b * pair + own : (b + 1) * pair])
            for b in range(chips)
        ],
        axis=1,
    )
    win_high[...], win_low[...] = halve(window)

    column = lax.broadcasted_iota(jnp.int32, (TILE, cols), 1)
    is_first, is_last = column == 0, column == cols - 1

    def along_cols(tile):
        after = jnp.where(is_last, 0.0, pltpu.roll(tile, cols - 1, 1))
        return after - jnp.where(is_first, 0.0, pltpu.roll(tile, 1, 1))

    def keep(where, field, value):
        top = value.astype(jnp.bfloat16)
        high[field, where, :] = top
        low[field, where, :] = (value - top.astype(jnp.float32)).astype(jnp.bfloat16)

    def smooth(field, weights):
        along[...] = dot_pair((ext_high[...], ext_low[...]), (high[field], low[field]))
        along[...] = dot_pair(halve(along[...]), (cols_high[...], cols_low[...]))

        @pl.loop(0, total // TILE, unroll=4)
        def _(t):
            tile = along[aligned(t * TILE, TILE), :]
            into = aligned(EDGE + t * TILE, TILE)
            for i in range(planes):
                vel[field, i, into, :] += weights[i] * tile

    def plane_weights(plane):
        return [-0.5 * smooth_z[i, plane] for i in range(planes)]

    def pass_on(plane):
        @pl.when(plane + ahead < planes)
        def _():
            send_own(plane + ahead)

        for distance in range(1, chips):

            @pl.when(chip >= distance)
            def _(distance=distance):
                arrived(plane, me - 2 * distance)
                if distance < chips - 1:

                    @pl.when(has_up)
                    def _():
                        up(plane, distance).start()

                side(plane, chip - distance).start()

            @pl.when(chip + distance < chips)
            def _(distance=distance):
                arrived(plane, me + 2 * distance)
                if distance < chips - 1:

                    @pl.when(has_down)
                    def _():
                        down(plane, distance).start()

                side(plane, chip + distance).start()

    def smooth_plane_fields(plane):
        for which in range(chips):
            arrived(plane, which * 2 + other)

        before = jnp.maximum(plane - 1, 0)
        far = jnp.maximum(plane - 2, 0)

        @pl.loop(0, rows // TILE, unroll=8)
        def _(t):
            here = aligned(PAD + t * TILE, TILE)
            into = aligned(t * TILE, TILE, TILE)
            wide_tile = raw[0, plane, aligned(EDGE + t * TILE, TILE + PAD), :]
            image, moment = wide_tile[EDGE : EDGE + TILE], raw[1, plane, here, :]
            keep(into, 0, moment * along_cols(image))
            keep(into, 1, moment * across(wide_tile))
            under = jnp.where(plane >= 2, raw[0, far, here, :], 0.0)
            keep(into, 2, raw[1, before, here, :] * (image - under))

        smooth(0, plane_weights(plane))
        smooth(1, plane_weights(plane))
        smooth(2, [jnp.where(plane >= 1, w, 0.0) for w in plane_weights(before)])

    lag = jnp.where(has_up & has_down, LAG, 0)

    @pl.loop(0, planes + LAG)
    def _(turn):
        @pl.when(turn < planes)
        def _():
            pass_on(turn)

        @pl.when((turn >= lag) & (turn < planes + lag))
        def _():
            smooth_plane_fields(turn - lag)

    last = planes - 1

    @pl.loop(0, rows // TILE, unroll=8)
    def _(t):
        here = aligned(PAD + t * TILE, TILE)
        keep(aligned(t * TILE, TILE, TILE), 2, raw[1, last, here, :] * (0.0 - raw[0, last - 1, here, :]))

    smooth(2, plane_weights(last))

    def part_copy(plane):
        return pltpu.make_async_remote_copy(
            src_ref=parts.at[plane % RING, :, aligned(other * own, span), :],
            dst_ref=swapped.at[plane],
            send_sem=part_send.at[plane], recv_sem=part_recv.at[plane],
            device_id={"slab": sibling}, device_id_type=MESH_ID,
        )

    @pl.loop(0, planes + 3)
    def _(turn):
        @pl.when(turn < planes)
        def _():
            plane = turn
            above, below = jnp.minimum(plane + 1, last), jnp.maximum(plane - 1, 0)

            @pl.loop(0, total // TILE, unroll=5)
            def _(t):
                b, k = t // (span // TILE), t % (span // TILE)
                g = b * pair + core * own + k * TILE + EDGE
                here, around = aligned(g, TILE), aligned(g - EDGE, TILE + PAD)
                at, at_around = aligned(t * TILE + EDGE, TILE), aligned(t * TILE, TILE + PAD)
                image_wide, moment_wide = raw[0, plane, around, :], raw[1, plane, around, :]
                image = image_wide[EDGE : EDGE + TILE]
                moment = moment_wide[EDGE : EDGE + TILE]
                row_wide = vel[1, plane, at_around, :]
                vel_c, vel_r = vel[0, plane, at, :], row_wide[EDGE : EDGE + TILE]
                vel_p = vel[2, plane, at, :]
                over = jnp.where(plane == last, 0.0, raw[0, above, here, :])
                under = jnp.where(plane == 0, 0.0, raw[0, below, here, :])
                push = (
                    vel_c * along_cols(image) + vel_r * across(image_wide) + vel_p * (over - under)
                )
                over = jnp.where(plane == last, 0.0, raw[1, above, here, :] * vel[2, above, at, :])
                under = jnp.where(plane == 0, 0.0, raw[1, below, here, :] * vel[2, below, at, :])
                flux = (
                    along_cols(moment * vel_c) + across(moment_wide * row_wide) + (over - under)
                )
                vel[0, plane, at, :] = image - scale * push
                moved[plane, aligned(t * TILE, TILE), :] = moment - scale * flux

        @pl.when((turn >= 1) & (turn <= planes))
        def _():
            plane = turn - 1
            above, below = jnp.minimum(plane + 1, last), jnp.maximum(plane - 1, 0)

            @pl.loop(0, half // TILE, unroll=8)
            def _(t):
                b, k = t // (own // TILE), t % (own // TILE)
                e = b * span + k * TILE + PAD
                at = aligned(e, TILE)
                into = aligned(t * TILE, TILE, TILE)
                image_wide = vel[0, plane, aligned(e - EDGE, TILE + PAD), :]
                image = image_wide[EDGE : EDGE + TILE]
                moment = moved[plane, aligned(e - EDGE, TILE), :]
                over = jnp.where(plane == last, 0.0, vel[0, above, at, :])
                under = jnp.where(plane == 0, 0.0, vel[0, below, at, :])
                keep(into, 0, moment * along_cols(image))
                keep(into, 1, moment * across(image_wide))
                keep(into, 2, moment * (over - under))

            @pl.when(plane >= RING)
            def _():
                part_copy(plane - RING).wait_send()

            inner = pl.ds(0, half)
            for field in range(3):
                parts[plane % RING, field] = dot_pair(
                    (win_high[...], win_low[...]), (high[field, inner, :], low[field, inner, :])
                )
            part_copy(plane).start()

        @pl.when(turn >= 3)
        def _():
            plane = turn - 3
            part_copy(plane).wait_recv()
            mine = aligned(core * own, span)
            both = parts[plane % RING, :, mine, :] + swapped[plane]
            out = dot_pair(halve(both.reshape(3 * span, cols)), (cols_high[...], cols_low[...]))
            swapped[plane] = out.reshape(3, span, cols)

    for plane in range(max(planes - RING, 0), planes):
        part_copy(plane).wait_send()

    subject_load = pltpu.make_async_copy(
        subjects.at[0], vel.at[2, :, pl.ds(own, own), :], local_sems.at[0]
    )
    subject_load.start()

    @pl.loop(0, 3 * (span // 8))
    def _(t):
        field, where = t // (span // 8), aligned((t % (span // 8)) * 8, 8)
        held = [swapped[j, field, where, :] for j in range(planes)]
        for i in range(planes):
            swapped[i, field, where, :] = -0.5 * sum(smooth_z[i, j] * held[j] for j in range(planes))

    subject_load.wait()

    image_at, moment_at, update_at = pl.ds(0, own), pl.ds(own, own), pl.ds(2 * own, own)
    sum_at, new_at = pl.ds(3 * own, own), pl.ds(4 * own, own)
    center_at, owned_at = pl.ds(0, own), pl.ds(2 * own, own)

    def pull_copy(plane, phase):
        source = vel.at[1, plane, update_at if phase == 0 else sum_at, :]
        by_x = plane % 2 == phase
        return pltpu.make_async_remote_copy(
            src_ref=source, dst_ref=(first_in, second_in)[phase].at[plane],
            send_sem=pull_send.at[phase, plane], recv_sem=pull_recv.at[phase, plane],
            device_id={"grp": jnp.where(by_x, across_x, across_y)}, device_id_type=MESH_ID,
        )

    @pl.loop(0, planes)
    def _(plane):
        above, below = jnp.minimum(plane + 1, last), jnp.maximum(plane - 1, 0)

        @pl.loop(0, own // TILE, unroll=4)
        def _(t):
            k = t * TILE
            e = chip * span + k + PAD
            at, around = aligned(e, TILE), aligned(e - EDGE, TILE + PAD)
            m_at, m_around = aligned(e - EDGE, TILE), aligned(e - PAD, TILE + PAD)
            v_at, v_around = aligned(k + EDGE, TILE), aligned(k, TILE + PAD)
            image_wide, moment_wide = vel[0, plane, around, :], moved[plane, m_around, :]
            image = image_wide[EDGE : EDGE + TILE]
            moment = moment_wide[EDGE : EDGE + TILE]
            row_wide = swapped[plane, 1, v_around, :]
            vel_c, vel_r = swapped[plane, 0, v_at, :], row_wide[EDGE : EDGE + TILE]
            vel_p = swapped[plane, 2, v_at, :]
            over = jnp.where(plane == last, 0.0, vel[0, above, at, :])
            under = jnp.where(plane == 0, 0.0, vel[0, below, at, :])
            push = vel_c * along_cols(image) + vel_r * across(image_wide) + vel_p * (over - under)
            over = jnp.where(
                plane == last, 0.0, moved[above, m_at, :] * swapped[above, 2, v_at, :]
            )
            under = jnp.where(plane == 0, 0.0, moved[below, m_at, :] * swapped[below, 2, v_at, :])
            flux = along_cols(moment * vel_c) + across(moment_wide * row_wide) + (over - under)
            new_image = image - scale * push
            vel[1, plane, aligned(k, TILE), :] = new_image
            vel[1, plane, aligned(own + k, TILE), :] = moment - scale * flux
            template = raw[0, plane, aligned(PAD + me * own + k, TILE), :]
            subject = vel[2, plane, aligned(own + k, TILE), :]
            vel[1, plane, aligned(2 * own + k, TILE), :] = template - learn_rate * (
                new_image - subject
            )

        pull_copy(plane, 0).start()

    stores = [
        pltpu.make_async_copy(vel.at[1, :, image_at, :], image_out.at[0], local_sems.at[1]),
        pltpu.make_async_copy(vel.at[1, :, moment_at, :], moment_out.at[0], local_sems.at[2]),
    ]
    for copy in stores:
        copy.start()

    @pl.loop(0, planes)
    def _(plane):
        pull_copy(plane, 0).wait_recv()
        vel[1, plane, sum_at, :] = vel[1, plane, update_at, :] + first_in[plane]
        pull_copy(plane, 1).start()

    @pl.loop(0, planes)
    def _(plane):
        pull_copy(plane, 1).wait_recv()
        center = (vel[1, plane, sum_at, :] + second_in[plane]) * 0.25
        update = vel[1, plane, update_at, :]
        vel[2, plane, center_at, :] = center
        vel[1, plane, new_at, :] = update + pull_weight * (center - update)

    stores.append(
        pltpu.make_async_copy(vel.at[1, :, new_at, :], template_out.at[0], local_sems.at[3])
    )
    stores[-1].start()
    block_planes = planes // 4
    mine = owned_block[grp]
    for k in range(block_planes):
        vel[2, k, owned_at, :] = vel[2, mine * block_planes + k, center_at, :]
    stores.append(
        pltpu.make_async_copy(
            vel.at[2, pl.ds(0, block_planes), owned_at, :], owned_out.at[0], local_sems.at[4]
        )
    )
    stores[-1].start()

    @pl.loop(0, planes)
    def _(plane):
        for distance in range(chips - 1):

            @pl.when(has_up & (chip >= distance))
            def _(distance=distance):
                up(plane, distance).wait_send()

            @pl.when(has_down & (chip + distance < chips))
            def _(distance=distance):
                down(plane, distance).wait_send()

        for which in range(chips):
            side(plane, which).wait_send()
        pull_copy(plane, 0).wait_send()
        pull_copy(plane, 1).wait_send()

    for copy in stores:
        copy.wait()


def on_device_whole(templates, momentum, subjects, smooth_x, smooth_y, smooth_z, owned_block):
    planes, own, cols = templates.shape[1:]
    rows = smooth_y.shape[0]
    chips = lax.axis_size("slab") // 2
    span, total = own + PAD, chips * (own + PAD)
    dims = (planes, rows, cols, own, chips)
    volume = jax.ShapeDtypeStruct(templates.shape, jnp.float32)
    owned = jax.ShapeDtypeStruct((1, planes // 4, own, cols), jnp.float32)
    any_space = pl.BlockSpec(memory_space=pl.ANY)
    smem = pl.BlockSpec(memory_space=pltpu.SMEM)
    f32 = lambda *shape: pltpu.VMEM(shape, jnp.float32)
    b16 = lambda *shape: pltpu.VMEM(shape, jnp.bfloat16)
    dma = lambda *shape: pltpu.SemaphoreType.DMA(shape)
    return pl.pallas_call(
        functools.partial(whole_kernel, dims),
        out_shape=(volume, volume, owned, volume),
        in_specs=[smem] * 2 + [any_space] * 5,
        out_specs=(any_space,) * 4,
        scratch_shapes=[
            f32(2, planes, rows + 2 * PAD, cols),
            f32(3, planes, total + PAD, cols),
            f32(planes, total, cols),
            b16(3, rows, cols),
            b16(3, rows, cols),
            f32(total, cols),
            f32(RING, 3, 2 * own + PAD, cols),
            f32(planes, 3, span, cols),
            f32(planes, own, cols),
            f32(planes, own, cols),
            f32(rows + PAD, cols),
            b16(total, rows),
            b16(total, rows),
            b16(cols, cols),
            b16(cols, cols),
            b16(2 * own + PAD, rows // 2),
            b16(2 * own + PAD, rows // 2),
            dma(5),
            dma(planes, chips - 1),
            dma(planes, chips - 1),
            dma(planes, chips),
            dma(planes, 2 * chips),
            dma(planes),
            dma(planes),
            dma(2, planes),
            dma(2, planes),
        ],
        compiler_params=pltpu.CompilerParams(
            collective_id=0, has_side_effects=True, vmem_limit_bytes=VMEM_LIMIT
        ),
        cost_estimate=pl.CostEstimate(
            flops=36 * planes * rows * rows * cols, bytes_accessed=2**24, transcendentals=0
        ),
    )(smooth_z, owned_block, templates, momentum, subjects, smooth_x, smooth_y)


def on_device(templates, momentum, subjects, smooth_x, smooth_y, smooth_z, owned_block):
    time_step = 1.0 / STEPS
    image = templates[0]
    moment = momentum[0]
    for section in range(STEPS):
        image_rows = with_halo(image, (("slab", 1),), 1)
        grad_rows = (image_rows[:, 2:, :] - image_rows[:, :-2, :]) * 0.5
        grad_cols = diff_cols(image)
        grad_planes = diff_planes(image)
        pushing = smooth_planes(
            jnp.stack([moment * grad_cols, moment * grad_rows, moment * grad_planes]), smooth_z
        )
        plane_fields = lax.all_to_all(pushing, "slab", split_axis=1, concat_axis=2, tiled=True)
        plane_vel = -smooth_plane(plane_fields, smooth_x, smooth_y)
        velocity = lax.all_to_all(plane_vel, "slab", split_axis=2, concat_axis=1, tiled=True)
        flux_edge = with_halo(moment * velocity[1], (("slab", 1),), 1)
        flux_rows = (flux_edge[:, 2:, :] - flux_edge[:, :-2, :]) * 0.5
        new_image = image - time_step * (
            velocity[0] * grad_cols + velocity[1] * grad_rows + velocity[2] * grad_planes
        )
        new_moment = moment - time_step * (
            diff_cols(moment * velocity[0]) + flux_rows + diff_planes(moment * velocity[2])
        )
        image = new_image
        moment = new_moment
    return finish(image, moment, templates, subjects, owned_block)


def finish(image, moment, templates, subjects, owned_block):
    update = templates[0] - learn_rate * (image - subjects[0])
    return (image[None], moment[None]) + pull(update, owned_block)


def sum_groups(field, orders):
    groups = lax.axis_size("grp")
    share = field.shape[0] // len(orders)
    pieces = [field[at * share : (at + 1) * share] for at in range(len(orders))]
    for turn in range(len(orders[0])):
        sent = [
            lax.ppermute(piece, "grp", [(i, i ^ order[turn]) for i in range(groups)])
            for piece, order in zip(pieces, orders)
        ]
        pieces = [piece + got for piece, got in zip(pieces, sent)]
    return jnp.concatenate(pieces, axis=0)


def pull(update, owned_block):
    groups = lax.axis_size("grp")
    planes_all = update.shape[0]
    block_planes = planes_all // groups
    if groups == 4 and planes_all % 2 == 0:
        center = sum_groups(update, ((1, 2), (2, 1))) / groups
    else:
        center = lax.psum(update, "grp") / groups
    owned_index = owned_block[lax.axis_index("grp")]
    owned_out = lax.dynamic_slice_in_dim(center, owned_index * block_planes, block_planes, 0)[None]
    new_template = update + pull_weight * (center - update)
    return (owned_out, new_template[None])


def solution(mesh):
    def body(*args):
        templates, smooth_y = args[0], args[4]
        gathered = 2 * 4 * templates.shape[1] * templates.shape[3] * smooth_y.shape[0]
        fits = gathered <= GATHER_BYTES and mesh.shape["grp"] == 4 and mesh.shape["slab"] % 2 == 0
        return (on_device_whole if fits else on_device)(*args)

    return jax.shard_map(
        body,
        mesh=mesh,
        in_specs=(
            P("grp", None, "slab", None),
            P("grp", None, "slab", None),
            P("grp", None, "slab", None),
            P(),
            P(),
            P(),
            P(),
        ),
        out_specs=(
            P("grp", None, "slab", None),
            P("grp", None, "slab", None),
            P("grp", None, "slab", None),
            P("grp", None, "slab", None),
        ),
        check_vma=False,
    )
```

```python
import functools

import jax
import jax.numpy as jnp
from jax import lax
from jax.experimental import pallas as pl
from jax.experimental.pallas import tpu as pltpu
from jax.sharding import PartitionSpec as P

STEPS = 2
GATHER_BYTES = 16 * 2**20
EDGE = 8
PAD = 2 * EDGE
TILE = 16
RING = 3
AHEAD = 3
LAG = 3
BEHIND = 2
HOP = 2
VMEM_LIMIT = 62 * 2**20
MESH_ID = pl.DeviceIdType.MESH


learn_rate = 0.5
pull_weight = 0.5


def with_halo(cells, sides, width):
    for axis, dim in sides:
        count = lax.axis_size(axis)
        ends = count - 1
        head = lax.slice_in_dim(cells, 0, width, axis=dim)
        tail = lax.slice_in_dim(cells, cells.shape[dim] - width, cells.shape[dim], axis=dim)
        cells = jnp.concatenate(
            [
                lax.ppermute(tail, axis, [(i, (i + 1) % count) for i in range(ends)]),
                cells,
                lax.ppermute(head, axis, [((i + 1) % count, i) for i in range(ends)]),
            ],
            axis=dim,
        )
    return cells


def diff_cols(field):
    zeros = jnp.zeros_like(field[..., :1])
    padded = jnp.concatenate([zeros, field, zeros], axis=-1)
    return (padded[..., 2:] - padded[..., :-2]) * 0.5


def diff_planes(field):
    zeros = jnp.zeros_like(field[..., :1, :, :])
    padded = jnp.concatenate([zeros, field, zeros], axis=-3)
    return (padded[..., 2:, :, :] - padded[..., :-2, :, :]) * 0.5


def smooth_planes(field, smooth_z):
    return jnp.einsum("ij,cjyx->ciyx", smooth_z, field, precision=lax.Precision.HIGHEST)


def smooth_plane(field, smooth_x, smooth_y):
    along = jnp.einsum("ij,cpyj->cpyi", smooth_x, field, precision=lax.Precision.HIGHEST)
    return jnp.einsum("ij,cpjx->cpix", smooth_y, along, precision=lax.Precision.HIGHEST)


def diff_rows(field):
    zeros = jnp.zeros_like(field[..., :1, :])
    padded = jnp.concatenate([zeros, field, zeros], axis=-2)
    return (padded[..., 2:, :] - padded[..., :-2, :]) * 0.5


def rows_of(field, start, count):
    return lax.dynamic_slice_in_dim(field, start, count, field.ndim - 2)


def halve(field):
    high = field.astype(jnp.bfloat16)
    return high, (field - high.astype(jnp.float32)).astype(jnp.bfloat16)


def dot_pair(left, right):
    mul = lambda a, b: jnp.dot(a, b, preferred_element_type=jnp.float32)
    return mul(left[0], right[0]) + (mul(left[0], right[1]) + mul(left[1], right[0]))


def aligned(start, size, step=8):
    return pl.ds(pl.multiple_of(start, step), size)


def across(wide):
    return wide[EDGE + 1 : EDGE + 1 + TILE] - wide[EDGE - 1 : EDGE - 1 + TILE]


def whole_kernel(
    dims, smooth_z, owned_block, templates, momentum, subjects, smooth_x, smooth_y,
    image_out, moment_out, owned_out, template_out,
    raw, vel, moved, high, low, along, parts, swapped, first_in, second_in, image_in,
    padded_y, ext_high, ext_low, cols_high, cols_low, win_high, win_low,
    local_sems, mate_sems, peer_sems, side_sems, recv_sems,
    part_send, part_recv, result_send, result_recv, pull_send, pull_recv, subject_sems,
):
    planes, rows, cols, own, chips = dims
    span = own + PAD
    pair = 2 * own
    half = rows // 2
    wide = 2 * pair + PAD
    me = lax.axis_index("slab")
    grp = lax.axis_index("grp")
    chip, core = me // 2, me % 2
    other = 1 - core
    sibling = chip * 2 + other
    middle = (chip == 1) | (chip == 2)
    is_end = (chip == 0) | (chip == 3)
    mate = jnp.where(chip % 2 == 0, me + 2, me - 2)
    peer = jnp.where(chip == 1, me + 2, jnp.where(chip == 2, me - 2, mate))
    peer_mate = jnp.where(chip == 1, me + 4, me - 4)
    scale = 0.5 / STEPS

    def own_rows(buffer_kind):
        return raw.at[buffer_kind, :, aligned(PAD + me * own, own), :]

    loads = [
        pltpu.make_async_copy(templates.at[0], own_rows(0), local_sems.at[0]),
        pltpu.make_async_copy(momentum.at[0], own_rows(1), local_sems.at[1]),
    ]
    mats = [
        pltpu.make_async_copy(smooth_y, padded_y.at[pl.ds(EDGE, rows), :], local_sems.at[2]),
        pltpu.make_async_copy(
            smooth_x.at[pl.ds(0, half), :], moved.at[0, pl.ds(0, half), :], local_sems.at[3]
        ),
        pltpu.make_async_copy(
            smooth_x.at[pl.ds(half, half), :], moved.at[1, pl.ds(0, half), :], local_sems.at[4]
        ),
    ]
    for copy in loads + mats:
        copy.start()

    barrier = pltpu.get_barrier_semaphore()

    def greet(where):
        pl.semaphore_signal(barrier, inc=1, device_id=where, device_id_type=MESH_ID)

    across_x = jnp.where(grp % 2 == 0, grp + 1, grp - 1)
    across_y = (grp + 2) % 4
    greet({"slab": mate})
    greet({"slab": sibling})
    greet({"grp": across_x})
    greet({"grp": across_y})

    @pl.when(middle)
    def _():
        greet({"slab": peer})

    pl.semaphore_wait(barrier, jnp.where(middle, 5, 4))

    for copy in loads:
        copy.wait()

    def send(plane, source, sem, target):
        piece = raw.at[:, plane, aligned(PAD + source * own, own), :]
        return pltpu.make_async_remote_copy(
            src_ref=piece, dst_ref=piece, send_sem=sem, recv_sem=recv_sems.at[plane, source],
            device_id={"slab": target}, device_id_type=MESH_ID,
        )

    def to_mate(plane, which):
        return send(plane, (me, peer, peer_mate)[which], mate_sems.at[plane, which], mate)

    def to_peer(plane, which):
        return send(plane, (me, mate)[which], peer_sems.at[plane, which], peer)

    def side(plane, source):
        return send(plane, source, side_sems.at[plane, source // 2], sibling)

    def arrived(plane, source):
        send(plane, source, side_sems.at[plane, 0], sibling).wait_recv()

    def send_own(plane):
        to_peer(plane, 0).start()
        side(plane, me).start()

    early = planes - 2

    ahead = min(AHEAD, planes)
    last = planes - 1
    lines = chips * span + PAD
    total = chips * span
    zeros_pad = jnp.zeros((PAD, cols), jnp.float32)
    column = lax.broadcasted_iota(jnp.int32, (TILE, cols), 1)
    is_first, is_last = column == 0, column == cols - 1

    def along_cols(tile):
        after = jnp.where(is_last, 0.0, pltpu.roll(tile, cols - 1, 1))
        return after - jnp.where(is_first, 0.0, pltpu.roll(tile, 1, 1))

    moment_at, update_at = pl.ds(own, own), pl.ds(2 * own, own)
    sum_at, new_at = pl.ds(3 * own, own), pl.ds(4 * own, own)
    center_at, owned_at = pl.ds(0, own), pl.ds(2 * own, own)
    mate_at = 3 * own

    def subject_load(plane):
        return pltpu.make_async_copy(
            subjects.at[0, plane], vel.at[1, plane, new_at, :], subject_sems.at[plane]
        )

    def result(plane):
        return pltpu.make_async_remote_copy(
            src_ref=vel.at[2, plane, pl.ds(mate_at, own), :], dst_ref=image_in.at[plane],
            send_sem=result_send.at[plane], recv_sem=result_recv.at[plane],
            device_id={"slab": mate}, device_id_type=MESH_ID,
        )

    def pull_copy(plane, phase):
        source = vel.at[1, plane, update_at if phase == 0 else sum_at, :]
        by_x = plane % 2 == phase
        return pltpu.make_async_remote_copy(
            src_ref=source, dst_ref=(first_in, second_in)[phase].at[plane],
            send_sem=pull_send.at[phase, plane], recv_sem=pull_recv.at[phase, plane],
            device_id={"grp": jnp.where(by_x, across_x, across_y)}, device_id_type=MESH_ID,
        )

    def pull_turn(turn):
        @pl.when(turn < planes)
        def _():
            plane = turn
            subject_load(plane).wait()

            @pl.when(is_end)
            def _():
                result(plane).wait_recv()

            template = raw[0, plane, aligned(PAD + me * own, own), :]
            subject = vel[1, plane, new_at, :]
            vel[1, plane, update_at, :] = template - learn_rate * (image_in[plane] - subject)
            pull_copy(plane, 0).start()

        @pl.when((turn >= HOP) & (turn < planes + HOP))
        def _():
            plane = turn - HOP
            pull_copy(plane, 0).wait_recv()
            vel[1, plane, sum_at, :] = vel[1, plane, update_at, :] + first_in[plane]
            pull_copy(plane, 1).start()

        @pl.when((turn >= 2 * HOP) & (turn < planes + 2 * HOP))
        def _():
            plane = turn - 2 * HOP
            pull_copy(plane, 1).wait_recv()
            center = (vel[1, plane, sum_at, :] + second_in[plane]) * 0.25
            update = vel[1, plane, update_at, :]
            vel[2, plane, center_at, :] = center
            vel[1, plane, new_at, :] = update + pull_weight * (center - update)

    @pl.when(is_end)
    def _():
        for plane in range(planes):
            to_mate(plane, 0).start()
        for plane in range(planes):
            side(plane, me).start()

    @pl.when(middle)
    def _():
        for plane in range(ahead):
            send_own(plane)

    from_mate = (mate, mate + (mate - me), mate + 2 * (mate - me))

    for kind in range(2):
        for plane in range(planes):
            raw[kind, plane, pl.ds(0, PAD), :] = zeros_pad
            raw[kind, plane, pl.ds(PAD + rows, PAD), :] = zeros_pad
    zeros_edge = jnp.zeros((EDGE, cols), jnp.float32)
    padded_y[pl.ds(0, EDGE), :] = zeros_edge
    padded_y[pl.ds(EDGE + rows, EDGE), :] = zeros_edge

    @pl.loop(0, 3 * planes)
    def _(at):
        @pl.loop(0, lines // TILE, unroll=3)
        def _(t):
            vel[at // planes, at % planes, aligned(t * TILE, TILE), :] = zeros_pad

    for copy in mats:
        copy.wait()
    turned = jnp.concatenate(
        [moved[0, pl.ds(0, half), :].T, moved[1, pl.ds(0, half), :].T], axis=1
    )
    cols_high[...], cols_low[...] = halve(turned)
    for b in range(chips):
        piece = padded_y[aligned(b * pair + core * own, span), :]
        ext_high[pl.ds(b * span, span), :], ext_low[pl.ds(b * span, span), :] = halve(piece)
    window = padded_y[aligned((chip // 2) * 2 * pair, wide), :]
    window = jnp.concatenate(
        [
            jnp.where(core == 0, window[:, b * pair : b * pair + own],
                      window[:, b * pair + own : (b + 1) * pair])
            for b in range(chips)
        ],
        axis=1,
    )
    win_high[...], win_low[...] = halve(window)

    def keep(where, field, value):
        top = value.astype(jnp.bfloat16)
        high[field, where, :] = top
        low[field, where, :] = (value - top.astype(jnp.float32)).astype(jnp.bfloat16)

    def smooth(field, weights):
        along[...] = dot_pair((ext_high[...], ext_low[...]), (high[field], low[field]))
        along[...] = dot_pair(halve(along[...]), (cols_high[...], cols_low[...]))

        @pl.loop(0, total // TILE, unroll=4)
        def _(t):
            tile = along[aligned(t * TILE, TILE), :]
            into = aligned(EDGE + t * TILE, TILE)
            for i in range(planes):
                vel[field, i, into, :] += weights[i] * tile

    def plane_weights(plane):
        return [-0.5 * smooth_z[i, plane] for i in range(planes)]

    def pass_on(plane):
        @pl.when(plane + ahead < planes)
        def _():
            send_own(plane + ahead)

        @pl.when(plane < early // 2)
        def _():
            to_mate(2 * plane, 0).start()
            to_mate(2 * plane + 1, 0).start()

        @pl.when(plane >= early)
        def _():
            to_mate(plane, 0).start()

        arrived(plane, mate)
        to_peer(plane, 1).start()
        side(plane, mate).start()

    def smooth_plane_fields(plane):
        @pl.when(middle)
        def _():
            for which, source in ((1, peer), (2, peer_mate)):
                arrived(plane, source)
                to_mate(plane, which).start()
                side(plane, source).start()

        @pl.when(is_end)
        def _():
            for source in from_mate:
                arrived(plane, source)
                side(plane, source).start()

        for which in range(chips):
            arrived(plane, which * 2 + other)

        before = jnp.maximum(plane - 1, 0)
        far = jnp.maximum(plane - 2, 0)

        @pl.loop(0, rows // TILE, unroll=8)
        def _(t):
            here = aligned(PAD + t * TILE, TILE)
            into = aligned(t * TILE, TILE, TILE)
            wide_tile = raw[0, plane, aligned(EDGE + t * TILE, TILE + PAD), :]
            image, moment = wide_tile[EDGE : EDGE + TILE], raw[1, plane, here, :]
            keep(into, 0, moment * along_cols(image))
            keep(into, 1, moment * across(wide_tile))
            under = jnp.where(plane >= 2, raw[0, far, here, :], 0.0)
            keep(into, 2, raw[1, before, here, :] * (image - under))

        smooth(0, plane_weights(plane))
        smooth(1, plane_weights(plane))
        smooth(2, [jnp.where(plane >= 1, w, 0.0) for w in plane_weights(before)])

    lag = jnp.where(middle, LAG, 0)

    @pl.loop(0, planes + LAG)
    def _(turn):
        @pl.when(middle & (turn < planes))
        def _():
            pass_on(turn)

        @pl.when((turn >= lag) & (turn < planes + lag))
        def _():
            smooth_plane_fields(turn - lag)

    @pl.loop(0, rows // TILE, unroll=8)
    def _(t):
        here = aligned(PAD + t * TILE, TILE)
        keep(aligned(t * TILE, TILE, TILE), 2, raw[1, last, here, :] * (0.0 - raw[0, last - 1, here, :]))

    smooth(2, plane_weights(last))

    def part_copy(plane, a):
        return pltpu.make_async_remote_copy(
            src_ref=parts.at[plane % RING, :, aligned(a * pair + other * own, span), :],
            dst_ref=swapped.at[plane, a],
            send_sem=part_send.at[plane, a], recv_sem=part_recv.at[plane, a],
            device_id={"slab": sibling}, device_id_type=MESH_ID,
        )

    needed = [middle | (chip % 2 == a) for a in range(2)]
    home_at = chip % 2

    @pl.loop(0, planes + 3)
    def _(turn):
        @pl.when(turn < planes)
        def _():
            plane = turn
            above, below = jnp.minimum(plane + 1, last), jnp.maximum(plane - 1, 0)

            @pl.loop(0, total // TILE, unroll=5)
            def _(t):
                b, k = t // (span // TILE), t % (span // TILE)
                g = b * pair + core * own + k * TILE + EDGE
                here, around = aligned(g, TILE), aligned(g - EDGE, TILE + PAD)
                at, at_around = aligned(t * TILE + EDGE, TILE), aligned(t * TILE, TILE + PAD)
                image_wide, moment_wide = raw[0, plane, around, :], raw[1, plane, around, :]
                image = image_wide[EDGE : EDGE + TILE]
                moment = moment_wide[EDGE : EDGE + TILE]
                row_wide = vel[1, plane, at_around, :]
                vel_c, vel_r = vel[0, plane, at, :], row_wide[EDGE : EDGE + TILE]
                vel_p = vel[2, plane, at, :]
                over = jnp.where(plane == last, 0.0, raw[0, above, here, :])
                under = jnp.where(plane == 0, 0.0, raw[0, below, here, :])
                push = (
                    vel_c * along_cols(image) + vel_r * across(image_wide) + vel_p * (over - under)
                )
                over = jnp.where(plane == last, 0.0, raw[1, above, here, :] * vel[2, above, at, :])
                under = jnp.where(plane == 0, 0.0, raw[1, below, here, :] * vel[2, below, at, :])
                flux = (
                    along_cols(moment * vel_c) + across(moment_wide * row_wide) + (over - under)
                )
                vel[0, plane, at, :] = image - scale * push
                moved[plane, aligned(t * TILE, TILE), :] = moment - scale * flux

        @pl.when((turn >= 1) & (turn <= planes))
        def _():
            plane = turn - 1
            above, below = jnp.minimum(plane + 1, last), jnp.maximum(plane - 1, 0)

            @pl.loop(0, half // TILE, unroll=8)
            def _(t):
                b, k = t // (own // TILE), t % (own // TILE)
                e = b * span + k * TILE + PAD
                at = aligned(e, TILE)
                into = aligned(t * TILE, TILE, TILE)
                image_wide = vel[0, plane, aligned(e - EDGE, TILE + PAD), :]
                image = image_wide[EDGE : EDGE + TILE]
                moment = moved[plane, aligned(e - EDGE, TILE), :]
                over = jnp.where(plane == last, 0.0, vel[0, above, at, :])
                under = jnp.where(plane == 0, 0.0, vel[0, below, at, :])
                keep(into, 0, moment * along_cols(image))
                keep(into, 1, moment * across(image_wide))
                keep(into, 2, moment * (over - under))

            @pl.when(plane >= RING)
            def _():
                for a in range(2):
                    @pl.when(needed[a])
                    def _(a=a):
                        part_copy(plane - RING, a).wait_send()

            inner = pl.ds(0, half)

            @pl.when(middle)
            def _():
                for field in range(3):
                    parts[plane % RING, field] = dot_pair(
                        (win_high[...], win_low[...]),
                        (high[field, inner, :], low[field, inner, :]),
                    )

            @pl.when(is_end)
            def _():
                lines_at = aligned(home_at * pair, pair + PAD, TILE)
                for field in range(3):
                    parts[plane % RING, field, lines_at, :] = dot_pair(
                        (win_high[lines_at, :], win_low[lines_at, :]),
                        (high[field, inner, :], low[field, inner, :]),
                    )

            for a in range(2):
                @pl.when(needed[a])
                def _(a=a):
                    part_copy(plane, a).start()

            subject_load(plane).start()

        @pl.when(turn >= 3)
        def _():
            plane = turn - 3
            for a in range(2):
                @pl.when(needed[a])
                def _(a=a):
                    part_copy(plane, a).wait_recv()
                    mine = parts[plane % RING, :, aligned(a * pair + core * own, span), :]
                    both = (mine + swapped[plane, a]).reshape(3 * span, cols)
                    out = dot_pair(halve(both), (cols_high[...], cols_low[...]))
                    swapped[plane, a] = out.reshape(3, span, cols)

        @pl.when(is_end & (turn >= BEHIND))
        def _():
            pull_turn(turn - BEHIND)

    for plane in range(max(planes - RING, 0), planes):
        for a in range(2):
            @pl.when(needed[a])
            def _(a=a):
                part_copy(plane, a).wait_send()

    def mix(a):
        @pl.loop(0, 3 * (span // 8), unroll=2)
        def _(t):
            field, where = t // (span // 8), aligned((t % (span // 8)) * 8, 8)
            held = [swapped[j, a, field, where, :] for j in range(planes)]
            for i in range(planes):
                swapped[i, a, field, where, :] = -0.5 * sum(
                    smooth_z[i, j] * held[j] for j in range(planes)
                )

    def last_rows(plane, home, keep_image, keep_moment):
        above, below = jnp.minimum(plane + 1, last), jnp.maximum(plane - 1, 0)
        a = home % 2

        @pl.loop(0, own // TILE, unroll=4)
        def _(t):
            k = t * TILE
            e = home * span + k + PAD
            at, around = aligned(e, TILE), aligned(e - EDGE, TILE + PAD)
            m_at, m_around = aligned(e - EDGE, TILE), aligned(e - PAD, TILE + PAD)
            v_at, v_around = aligned(k + EDGE, TILE), aligned(k, TILE + PAD)
            image_wide, moment_wide = vel[0, plane, around, :], moved[plane, m_around, :]
            image = image_wide[EDGE : EDGE + TILE]
            moment = moment_wide[EDGE : EDGE + TILE]
            row_wide = swapped[plane, a, 1, v_around, :]
            vel_c, vel_r = swapped[plane, a, 0, v_at, :], row_wide[EDGE : EDGE + TILE]
            vel_p = swapped[plane, a, 2, v_at, :]
            if keep_image is not None:
                over = jnp.where(plane == last, 0.0, vel[0, above, at, :])
                under = jnp.where(plane == 0, 0.0, vel[0, below, at, :])
                push = vel_c * along_cols(image) + vel_r * across(image_wide)
                keep_image(plane, k, image - scale * (push + vel_p * (over - under)))
            if keep_moment:
                over = moved[above, m_at, :] * swapped[above, a, 2, v_at, :]
                under = moved[below, m_at, :] * swapped[below, a, 2, v_at, :]
                over = jnp.where(plane == last, 0.0, over)
                under = jnp.where(plane == 0, 0.0, under)
                flux = along_cols(moment * vel_c) + across(moment_wide * row_wide) + (over - under)
                vel[1, plane, aligned(own + k, TILE), :] = moment - scale * flux

    def to_send(plane, k, value):
        vel[2, plane, aligned(mate_at + k, TILE), :] = value

    def to_keep(plane, k, value):
        image_in[plane, aligned(k, TILE), :] = value

    @pl.when(middle)
    def _():
        mix(1 - home_at)

        @pl.loop(0, planes)
        def _(plane):
            last_rows(plane, mate // 2, to_send, False)
            result(plane).start()

        mix(home_at)

        @pl.loop(0, planes)
        def _(plane):
            last_rows(plane, chip, to_keep, True)
            pull_turn(plane)

        @pl.loop(planes, planes + 2 * HOP)
        def _(turn):
            pull_turn(turn)

    @pl.when(is_end)
    def _():
        mix(home_at)

        @pl.loop(0, planes)
        def _(plane):
            last_rows(plane, chip, None, True)

        @pl.loop(planes + 3 - BEHIND, planes + 2 * HOP)
        def _(turn):
            pull_turn(turn)

    stores = [
        pltpu.make_async_copy(image_in, image_out.at[0], local_sems.at[1]),
        pltpu.make_async_copy(vel.at[1, :, moment_at, :], moment_out.at[0], local_sems.at[2]),
    ]
    for copy in stores:
        copy.start()

    stores.append(
        pltpu.make_async_copy(vel.at[1, :, new_at, :], template_out.at[0], local_sems.at[3])
    )
    stores[-1].start()
    block_planes = planes // 4
    mine = owned_block[grp]
    for k in range(block_planes):
        vel[2, k, owned_at, :] = vel[2, mine * block_planes + k, center_at, :]
    stores.append(
        pltpu.make_async_copy(
            vel.at[2, pl.ds(0, block_planes), owned_at, :], owned_out.at[0], local_sems.at[4]
        )
    )
    stores[-1].start()

    @pl.loop(0, planes)
    def _(plane):
        pull_copy(plane, 0).wait_send()
        pull_copy(plane, 1).wait_send()
        to_mate(plane, 0).wait_send()
        for which in range(chips):
            side(plane, which * 2 + core).wait_send()

        @pl.when(middle)
        def _():
            to_peer(plane, 0).wait_send()
            to_peer(plane, 1).wait_send()
            to_mate(plane, 1).wait_send()
            to_mate(plane, 2).wait_send()
            result(plane).wait_send()

    for copy in stores:
        copy.wait()


def on_device_whole(templates, momentum, subjects, smooth_x, smooth_y, smooth_z, owned_block):
    planes, own, cols = templates.shape[1:]
    rows = smooth_y.shape[0]
    chips = lax.axis_size("slab") // 2
    span, total = own + PAD, chips * (own + PAD)
    dims = (planes, rows, cols, own, chips)
    volume = jax.ShapeDtypeStruct(templates.shape, jnp.float32)
    owned = jax.ShapeDtypeStruct((1, planes // 4, own, cols), jnp.float32)
    any_space = pl.BlockSpec(memory_space=pl.ANY)
    smem = pl.BlockSpec(memory_space=pltpu.SMEM)
    f32 = lambda *shape: pltpu.VMEM(shape, jnp.float32)
    b16 = lambda *shape: pltpu.VMEM(shape, jnp.bfloat16)
    dma = lambda *shape: pltpu.SemaphoreType.DMA(shape)
    return pl.pallas_call(
        functools.partial(whole_kernel, dims),
        out_shape=(volume, volume, owned, volume),
        in_specs=[smem] * 2 + [any_space] * 5,
        out_specs=(any_space,) * 4,
        scratch_shapes=[
            f32(2, planes, rows + 2 * PAD, cols),
            f32(3, planes, total + PAD, cols),
            f32(planes, total, cols),
            b16(3, rows, cols),
            b16(3, rows, cols),
            f32(total, cols),
            f32(RING, 3, 4 * own + PAD, cols),
            f32(planes, 2, 3, span, cols),
            f32(planes, own, cols),
            f32(planes, own, cols),
            f32(planes, own, cols),
            f32(rows + PAD, cols),
            b16(total, rows),
            b16(total, rows),
            b16(cols, cols),
            b16(cols, cols),
            b16(4 * own + PAD, rows // 2),
            b16(4 * own + PAD, rows // 2),
            dma(5),
            dma(planes, 3),
            dma(planes, 2),
            dma(planes, chips),
            dma(planes, 2 * chips),
            dma(planes, 2),
            dma(planes, 2),
            dma(planes),
            dma(planes),
            dma(2, planes),
            dma(2, planes),
            dma(planes),
        ],
        compiler_params=pltpu.CompilerParams(
            collective_id=0, has_side_effects=True, vmem_limit_bytes=VMEM_LIMIT
        ),
        cost_estimate=pl.CostEstimate(
            flops=36 * planes * rows * rows * cols, bytes_accessed=2**24, transcendentals=0
        ),
    )(smooth_z, owned_block, templates, momentum, subjects, smooth_x, smooth_y)


def on_device(templates, momentum, subjects, smooth_x, smooth_y, smooth_z, owned_block):
    time_step = 1.0 / STEPS
    image = templates[0]
    moment = momentum[0]
    for section in range(STEPS):
        image_rows = with_halo(image, (("slab", 1),), 1)
        grad_rows = (image_rows[:, 2:, :] - image_rows[:, :-2, :]) * 0.5
        grad_cols = diff_cols(image)
        grad_planes = diff_planes(image)
        pushing = smooth_planes(
            jnp.stack([moment * grad_cols, moment * grad_rows, moment * grad_planes]), smooth_z
        )
        plane_fields = lax.all_to_all(pushing, "slab", split_axis=1, concat_axis=2, tiled=True)
        plane_vel = -smooth_plane(plane_fields, smooth_x, smooth_y)
        velocity = lax.all_to_all(plane_vel, "slab", split_axis=2, concat_axis=1, tiled=True)
        flux_edge = with_halo(moment * velocity[1], (("slab", 1),), 1)
        flux_rows = (flux_edge[:, 2:, :] - flux_edge[:, :-2, :]) * 0.5
        new_image = image - time_step * (
            velocity[0] * grad_cols + velocity[1] * grad_rows + velocity[2] * grad_planes
        )
        new_moment = moment - time_step * (
            diff_cols(moment * velocity[0]) + flux_rows + diff_planes(moment * velocity[2])
        )
        image = new_image
        moment = new_moment
    return finish(image, moment, templates, subjects, owned_block)


def finish(image, moment, templates, subjects, owned_block):
    update = templates[0] - learn_rate * (image - subjects[0])
    return (image[None], moment[None]) + pull(update, owned_block)


def sum_groups(field, orders):
    groups = lax.axis_size("grp")
    share = field.shape[0] // len(orders)
    pieces = [field[at * share : (at + 1) * share] for at in range(len(orders))]
    for turn in range(len(orders[0])):
        sent = [
            lax.ppermute(piece, "grp", [(i, i ^ order[turn]) for i in range(groups)])
            for piece, order in zip(pieces, orders)
        ]
        pieces = [piece + got for piece, got in zip(pieces, sent)]
    return jnp.concatenate(pieces, axis=0)


def pull(update, owned_block):
    groups = lax.axis_size("grp")
    planes_all = update.shape[0]
    block_planes = planes_all // groups
    if groups == 4 and planes_all % 2 == 0:
        center = sum_groups(update, ((1, 2), (2, 1))) / groups
    else:
        center = lax.psum(update, "grp") / groups
    owned_index = owned_block[lax.axis_index("grp")]
    owned_out = lax.dynamic_slice_in_dim(center, owned_index * block_planes, block_planes, 0)[None]
    new_template = update + pull_weight * (center - update)
    return (owned_out, new_template[None])


def solution(mesh):
    def body(*args):
        templates, smooth_y = args[0], args[4]
        gathered = 2 * 4 * templates.shape[1] * templates.shape[3] * smooth_y.shape[0]
        fits = gathered <= GATHER_BYTES and mesh.shape["grp"] == 4 and mesh.shape["slab"] == 8
        return (on_device_whole if fits else on_device)(*args)

    return jax.shard_map(
        body,
        mesh=mesh,
        in_specs=(
            P("grp", None, "slab", None),
            P("grp", None, "slab", None),
            P("grp", None, "slab", None),
            P(),
            P(),
            P(),
            P(),
        ),
        out_specs=(
            P("grp", None, "slab", None),
            P("grp", None, "slab", None),
            P("grp", None, "slab", None),
            P("grp", None, "slab", None),
        ),
        check_vma=False,
    )
```

```python
import functools

import jax
import jax.numpy as jnp
from jax import lax
from jax.experimental import pallas as pl
from jax.experimental.pallas import tpu as pltpu
from jax.sharding import PartitionSpec as P

STEPS = 2
GATHER_BYTES = 16 * 2**20
EDGE = 8
PAD = 2 * EDGE
TILE = 16
RING = 3
AHEAD = 3
LAG = 3
BEHIND = 2
HOP = 2
VMEM_LIMIT = 62 * 2**20
MESH_ID = pl.DeviceIdType.MESH


learn_rate = 0.5
pull_weight = 0.5


def with_halo(cells, sides, width):
    for axis, dim in sides:
        count = lax.axis_size(axis)
        ends = count - 1
        head = lax.slice_in_dim(cells, 0, width, axis=dim)
        tail = lax.slice_in_dim(cells, cells.shape[dim] - width, cells.shape[dim], axis=dim)
        cells = jnp.concatenate(
            [
                lax.ppermute(tail, axis, [(i, (i + 1) % count) for i in range(ends)]),
                cells,
                lax.ppermute(head, axis, [((i + 1) % count, i) for i in range(ends)]),
            ],
            axis=dim,
        )
    return cells


def diff_cols(field):
    zeros = jnp.zeros_like(field[..., :1])
    padded = jnp.concatenate([zeros, field, zeros], axis=-1)
    return (padded[..., 2:] - padded[..., :-2]) * 0.5


def diff_planes(field):
    zeros = jnp.zeros_like(field[..., :1, :, :])
    padded = jnp.concatenate([zeros, field, zeros], axis=-3)
    return (padded[..., 2:, :, :] - padded[..., :-2, :, :]) * 0.5


def smooth_planes(field, smooth_z):
    return jnp.einsum("ij,cjyx->ciyx", smooth_z, field, precision=lax.Precision.HIGHEST)


def smooth_plane(field, smooth_x, smooth_y):
    along = jnp.einsum("ij,cpyj->cpyi", smooth_x, field, precision=lax.Precision.HIGHEST)
    return jnp.einsum("ij,cpjx->cpix", smooth_y, along, precision=lax.Precision.HIGHEST)


def diff_rows(field):
    zeros = jnp.zeros_like(field[..., :1, :])
    padded = jnp.concatenate([zeros, field, zeros], axis=-2)
    return (padded[..., 2:, :] - padded[..., :-2, :]) * 0.5


def rows_of(field, start, count):
    return lax.dynamic_slice_in_dim(field, start, count, field.ndim - 2)


def halve(field):
    high = field.astype(jnp.bfloat16)
    return high, (field - high.astype(jnp.float32)).astype(jnp.bfloat16)


def dot_pair(left, right):
    mul = lambda a, b: jnp.dot(a, b, preferred_element_type=jnp.float32)
    return mul(left[0], right[0]) + (mul(left[0], right[1]) + mul(left[1], right[0]))


def aligned(start, size, step=8):
    return pl.ds(pl.multiple_of(start, step), size)


def across(wide):
    return wide[EDGE + 1 : EDGE + 1 + TILE] - wide[EDGE - 1 : EDGE - 1 + TILE]


def whole_kernel(
    dims, smooth_z, owned_block, templates, momentum, subjects, smooth_x, smooth_y,
    image_out, moment_out, owned_out, template_out,
    raw, vel, moved, high, low, along, parts, swapped, first_in, second_in, image_in,
    padded_y, ext_high, ext_low, cols_high, cols_low, win_high, win_low,
    local_sems, mate_sems, peer_sems, side_sems, recv_sems,
    part_send, part_recv, result_send, result_recv, pull_send, pull_recv, subject_sems,
):
    planes, rows, cols, own, chips = dims
    span = own + PAD
    pair = 2 * own
    half = rows // 2
    wide = 2 * pair + PAD
    me = lax.axis_index("slab")
    grp = lax.axis_index("grp")
    chip, core = me // 2, me % 2
    other = 1 - core
    sibling = chip * 2 + other
    middle = (chip == 1) | (chip == 2)
    is_end = (chip == 0) | (chip == 3)
    mate = jnp.where(chip % 2 == 0, me + 2, me - 2)
    peer = jnp.where(chip == 1, me + 2, jnp.where(chip == 2, me - 2, mate))
    peer_mate = jnp.where(chip == 1, me + 4, me - 4)
    scale = 0.5 / STEPS

    def own_rows(buffer_kind):
        return raw.at[buffer_kind, :, aligned(PAD + me * own, own), :]

    loads = [
        pltpu.make_async_copy(templates.at[0], own_rows(0), local_sems.at[0]),
        pltpu.make_async_copy(momentum.at[0], own_rows(1), local_sems.at[1]),
    ]
    mats = [
        pltpu.make_async_copy(smooth_y, padded_y.at[pl.ds(EDGE, rows), :], local_sems.at[2]),
        pltpu.make_async_copy(
            smooth_x.at[pl.ds(0, half), :], moved.at[0, pl.ds(0, half), :], local_sems.at[3]
        ),
        pltpu.make_async_copy(
            smooth_x.at[pl.ds(half, half), :], moved.at[1, pl.ds(0, half), :], local_sems.at[4]
        ),
    ]
    for copy in loads + mats:
        copy.start()

    barrier = pltpu.get_barrier_semaphore()

    def greet(where):
        pl.semaphore_signal(barrier, inc=1, device_id=where, device_id_type=MESH_ID)

    across_x = jnp.where(grp % 2 == 0, grp + 1, grp - 1)
    across_y = (grp + 2) % 4
    greet({"slab": mate})
    greet({"slab": sibling})
    greet({"grp": across_x})
    greet({"grp": across_y})

    @pl.when(middle)
    def _():
        greet({"slab": peer})

    pl.semaphore_wait(barrier, jnp.where(middle, 5, 4))

    for copy in loads:
        copy.wait()

    def send(plane, source, sem, target):
        piece = raw.at[:, plane, aligned(PAD + source * own, own), :]
        return pltpu.make_async_remote_copy(
            src_ref=piece, dst_ref=piece, send_sem=sem, recv_sem=recv_sems.at[plane, source],
            device_id={"slab": target}, device_id_type=MESH_ID,
        )

    def to_mate(plane, which):
        return send(plane, (me, peer, peer_mate)[which], mate_sems.at[plane, which], mate)

    def to_peer(plane, which):
        return send(plane, (me, mate)[which], peer_sems.at[plane, which], peer)

    def side(plane, source):
        return send(plane, source, side_sems.at[plane, source // 2], sibling)

    def arrived(plane, source):
        send(plane, source, side_sems.at[plane, 0], sibling).wait_recv()

    def send_own(plane):
        to_peer(plane, 0).start()
        side(plane, me).start()

    early = planes - 2

    ahead = min(AHEAD, planes)
    last = planes - 1
    lines = chips * span + PAD
    total = chips * span
    zeros_pad = jnp.zeros((PAD, cols), jnp.float32)
    column = lax.broadcasted_iota(jnp.int32, (TILE, cols), 1)
    is_first, is_last = column == 0, column == cols - 1

    def along_cols(tile):
        after = jnp.where(is_last, 0.0, pltpu.roll(tile, cols - 1, 1))
        return after - jnp.where(is_first, 0.0, pltpu.roll(tile, 1, 1))

    moment_at, update_at = pl.ds(own, own), pl.ds(2 * own, own)
    sum_at, new_at = pl.ds(3 * own, own), pl.ds(4 * own, own)
    center_at, owned_at = pl.ds(0, own), pl.ds(2 * own, own)
    mate_at = 3 * own

    def subject_load(plane):
        return pltpu.make_async_copy(
            subjects.at[0, plane], vel.at[1, plane, new_at, :], subject_sems.at[plane]
        )

    def result(plane):
        return pltpu.make_async_remote_copy(
            src_ref=vel.at[2, plane, pl.ds(mate_at, own), :], dst_ref=image_in.at[plane],
            send_sem=result_send.at[plane], recv_sem=result_recv.at[plane],
            device_id={"slab": mate}, device_id_type=MESH_ID,
        )

    def pull_copy(plane, phase):
        source = vel.at[1, plane, update_at if phase == 0 else sum_at, :]
        by_x = plane % 2 == phase
        return pltpu.make_async_remote_copy(
            src_ref=source, dst_ref=(first_in, second_in)[phase].at[plane],
            send_sem=pull_send.at[phase, plane], recv_sem=pull_recv.at[phase, plane],
            device_id={"grp": jnp.where(by_x, across_x, across_y)}, device_id_type=MESH_ID,
        )

    def pull_turn(turn):
        @pl.when(turn < planes)
        def _():
            plane = turn
            subject_load(plane).wait()

            @pl.when(is_end)
            def _():
                result(plane).wait_recv()

            template = raw[0, plane, aligned(PAD + me * own, own), :]
            subject = vel[1, plane, new_at, :]
            vel[1, plane, update_at, :] = template - learn_rate * (image_in[plane] - subject)
            pull_copy(plane, 0).start()

        @pl.when((turn >= HOP) & (turn < planes + HOP))
        def _():
            plane = turn - HOP
            pull_copy(plane, 0).wait_recv()
            vel[1, plane, sum_at, :] = vel[1, plane, update_at, :] + first_in[plane]
            pull_copy(plane, 1).start()

        @pl.when((turn >= 2 * HOP) & (turn < planes + 2 * HOP))
        def _():
            plane = turn - 2 * HOP
            pull_copy(plane, 1).wait_recv()
            center = (vel[1, plane, sum_at, :] + second_in[plane]) * 0.25
            update = vel[1, plane, update_at, :]
            vel[2, plane, center_at, :] = center
            vel[1, plane, new_at, :] = update + pull_weight * (center - update)

    @pl.when(is_end)
    def _():
        for plane in range(planes):
            to_mate(plane, 0).start()
        for plane in range(planes):
            side(plane, me).start()

    @pl.when(middle)
    def _():
        for plane in range(ahead):
            send_own(plane)
        for plane in range(2):
            to_mate(plane, 0).start()

    from_mate = (mate, mate + (mate - me), mate + 2 * (mate - me))

    for kind in range(2):
        for plane in range(planes):
            raw[kind, plane, pl.ds(0, PAD), :] = zeros_pad
            raw[kind, plane, pl.ds(PAD + rows, PAD), :] = zeros_pad
    zeros_edge = jnp.zeros((EDGE, cols), jnp.float32)
    padded_y[pl.ds(0, EDGE), :] = zeros_edge
    padded_y[pl.ds(EDGE + rows, EDGE), :] = zeros_edge

    @pl.loop(0, 3 * planes)
    def _(at):
        @pl.loop(0, lines // TILE, unroll=3)
        def _(t):
            vel[at // planes, at % planes, aligned(t * TILE, TILE), :] = zeros_pad

    for copy in mats:
        copy.wait()
    turned = jnp.concatenate(
        [moved[0, pl.ds(0, half), :].T, moved[1, pl.ds(0, half), :].T], axis=1
    )
    cols_high[...], cols_low[...] = halve(turned)
    for b in range(chips):
        piece = padded_y[aligned(b * pair + core * own, span), :]
        ext_high[pl.ds(b * span, span), :], ext_low[pl.ds(b * span, span), :] = halve(piece)
    window = padded_y[aligned((chip // 2) * 2 * pair, wide), :]
    window = jnp.concatenate(
        [
            jnp.where(core == 0, window[:, b * pair : b * pair + own],
                      window[:, b * pair + own : (b + 1) * pair])
            for b in range(chips)
        ],
        axis=1,
    )
    win_high[...], win_low[...] = halve(window)

    def keep(where, field, value):
        top = value.astype(jnp.bfloat16)
        high[field, where, :] = top
        low[field, where, :] = (value - top.astype(jnp.float32)).astype(jnp.bfloat16)

    def smooth(field, weights):
        along[...] = dot_pair((ext_high[...], ext_low[...]), (high[field], low[field]))
        along[...] = dot_pair(halve(along[...]), (cols_high[...], cols_low[...]))

        @pl.loop(0, total // TILE, unroll=4)
        def _(t):
            tile = along[aligned(t * TILE, TILE), :]
            into = aligned(EDGE + t * TILE, TILE)
            for i in range(planes):
                vel[field, i, into, :] += weights[i] * tile

    def plane_weights(plane):
        return [-0.5 * smooth_z[i, plane] for i in range(planes)]

    def pass_on(plane):
        @pl.when(plane + ahead < planes)
        def _():
            send_own(plane + ahead)

        @pl.when(plane < early // 2 - 1)
        def _():
            to_mate(2 * plane + 2, 0).start()
            to_mate(2 * plane + 3, 0).start()

        @pl.when(plane >= early)
        def _():
            to_mate(plane, 0).start()

        arrived(plane, mate)
        to_peer(plane, 1).start()
        side(plane, mate).start()

    def smooth_plane_fields(plane):
        @pl.when(middle)
        def _():
            for which, source in ((1, peer), (2, peer_mate)):
                arrived(plane, source)
                to_mate(plane, which).start()
                side(plane, source).start()

        @pl.when(is_end)
        def _():
            for source in from_mate:
                arrived(plane, source)
                side(plane, source).start()

        for which in range(chips):
            arrived(plane, which * 2 + other)

        before = jnp.maximum(plane - 1, 0)
        far = jnp.maximum(plane - 2, 0)

        @pl.loop(0, rows // TILE, unroll=8)
        def _(t):
            here = aligned(PAD + t * TILE, TILE)
            into = aligned(t * TILE, TILE, TILE)
            wide_tile = raw[0, plane, aligned(EDGE + t * TILE, TILE + PAD), :]
            image, moment = wide_tile[EDGE : EDGE + TILE], raw[1, plane, here, :]
            keep(into, 0, moment * along_cols(image))
            keep(into, 1, moment * across(wide_tile))
            under = jnp.where(plane >= 2, raw[0, far, here, :], 0.0)
            keep(into, 2, raw[1, before, here, :] * (image - under))

        smooth(0, plane_weights(plane))
        smooth(1, plane_weights(plane))
        smooth(2, [jnp.where(plane >= 1, w, 0.0) for w in plane_weights(before)])

    lag = jnp.where(middle, LAG, 0)

    @pl.loop(0, planes + LAG)
    def _(turn):
        @pl.when(middle & (turn < planes))
        def _():
            pass_on(turn)

        @pl.when((turn >= lag) & (turn < planes + lag))
        def _():
            smooth_plane_fields(turn - lag)

    @pl.loop(0, rows // TILE, unroll=8)
    def _(t):
        here = aligned(PAD + t * TILE, TILE)
        keep(aligned(t * TILE, TILE, TILE), 2, raw[1, last, here, :] * (0.0 - raw[0, last - 1, here, :]))

    smooth(2, plane_weights(last))

    def part_copy(plane, a):
        return pltpu.make_async_remote_copy(
            src_ref=parts.at[plane % RING, :, aligned(a * pair + other * own, span), :],
            dst_ref=swapped.at[plane, a],
            send_sem=part_send.at[plane, a], recv_sem=part_recv.at[plane, a],
            device_id={"slab": sibling}, device_id_type=MESH_ID,
        )

    needed = [middle | (chip % 2 == a) for a in range(2)]
    home_at = chip % 2

    @pl.loop(0, planes + 3)
    def _(turn):
        @pl.when(turn < planes)
        def _():
            plane = turn
            above, below = jnp.minimum(plane + 1, last), jnp.maximum(plane - 1, 0)

            @pl.loop(0, total // TILE, unroll=5)
            def _(t):
                b, k = t // (span // TILE), t % (span // TILE)
                g = b * pair + core * own + k * TILE + EDGE
                here, around = aligned(g, TILE), aligned(g - EDGE, TILE + PAD)
                at, at_around = aligned(t * TILE + EDGE, TILE), aligned(t * TILE, TILE + PAD)
                image_wide, moment_wide = raw[0, plane, around, :], raw[1, plane, around, :]
                image = image_wide[EDGE : EDGE + TILE]
                moment = moment_wide[EDGE : EDGE + TILE]
                row_wide = vel[1, plane, at_around, :]
                vel_c, vel_r = vel[0, plane, at, :], row_wide[EDGE : EDGE + TILE]
                vel_p = vel[2, plane, at, :]
                over = jnp.where(plane == last, 0.0, raw[0, above, here, :])
                under = jnp.where(plane == 0, 0.0, raw[0, below, here, :])
                push = (
                    vel_c * along_cols(image) + vel_r * across(image_wide) + vel_p * (over - under)
                )
                over = jnp.where(plane == last, 0.0, raw[1, above, here, :] * vel[2, above, at, :])
                under = jnp.where(plane == 0, 0.0, raw[1, below, here, :] * vel[2, below, at, :])
                flux = (
                    along_cols(moment * vel_c) + across(moment_wide * row_wide) + (over - under)
                )
                vel[0, plane, at, :] = image - scale * push
                moved[plane, aligned(t * TILE, TILE), :] = moment - scale * flux

        @pl.when((turn >= 1) & (turn <= planes))
        def _():
            plane = turn - 1
            above, below = jnp.minimum(plane + 1, last), jnp.maximum(plane - 1, 0)

            @pl.loop(0, half // TILE, unroll=8)
            def _(t):
                b, k = t // (own // TILE), t % (own // TILE)
                e = b * span + k * TILE + PAD
                at = aligned(e, TILE)
                into = aligned(t * TILE, TILE, TILE)
                image_wide = vel[0, plane, aligned(e - EDGE, TILE + PAD), :]
                image = image_wide[EDGE : EDGE + TILE]
                moment = moved[plane, aligned(e - EDGE, TILE), :]
                over = jnp.where(plane == last, 0.0, vel[0, above, at, :])
                under = jnp.where(plane == 0, 0.0, vel[0, below, at, :])
                keep(into, 0, moment * along_cols(image))
                keep(into, 1, moment * across(image_wide))
                keep(into, 2, moment * (over - under))

            @pl.when(plane >= RING)
            def _():
                for a in range(2):
                    @pl.when(needed[a])
                    def _(a=a):
                        part_copy(plane - RING, a).wait_send()

            inner = pl.ds(0, half)

            @pl.when(middle)
            def _():
                for field in range(3):
                    parts[plane % RING, field] = dot_pair(
                        (win_high[...], win_low[...]),
                        (high[field, inner, :], low[field, inner, :]),
                    )

            @pl.when(is_end)
            def _():
                lines_at = aligned(home_at * pair, pair + PAD, TILE)
                for field in range(3):
                    parts[plane % RING, field, lines_at, :] = dot_pair(
                        (win_high[lines_at, :], win_low[lines_at, :]),
                        (high[field, inner, :], low[field, inner, :]),
                    )

            for a in range(2):
                @pl.when(needed[a])
                def _(a=a):
                    part_copy(plane, a).start()

            subject_load(plane).start()

        @pl.when(turn >= 3)
        def _():
            plane = turn - 3
            for a in range(2):
                @pl.when(needed[a])
                def _(a=a):
                    part_copy(plane, a).wait_recv()
                    mine = parts[plane % RING, :, aligned(a * pair + core * own, span), :]
                    both = (mine + swapped[plane, a]).reshape(3 * span, cols)
                    out = dot_pair(halve(both), (cols_high[...], cols_low[...]))
                    swapped[plane, a] = out.reshape(3, span, cols)

        @pl.when(is_end & (turn >= BEHIND))
        def _():
            pull_turn(turn - BEHIND)

    for plane in range(max(planes - RING, 0), planes):
        for a in range(2):
            @pl.when(needed[a])
            def _(a=a):
                part_copy(plane, a).wait_send()

    def mix(a):
        @pl.loop(0, 3 * (span // 8), unroll=2)
        def _(t):
            field, where = t // (span // 8), aligned((t % (span // 8)) * 8, 8)
            held = [swapped[j, a, field, where, :] for j in range(planes)]
            for i in range(planes):
                swapped[i, a, field, where, :] = -0.5 * sum(
                    smooth_z[i, j] * held[j] for j in range(planes)
                )

    def last_rows(plane, home, keep_image, keep_moment):
        above, below = jnp.minimum(plane + 1, last), jnp.maximum(plane - 1, 0)
        a = home % 2

        @pl.loop(0, own // TILE, unroll=4)
        def _(t):
            k = t * TILE
            e = home * span + k + PAD
            at, around = aligned(e, TILE), aligned(e - EDGE, TILE + PAD)
            m_at, m_around = aligned(e - EDGE, TILE), aligned(e - PAD, TILE + PAD)
            v_at, v_around = aligned(k + EDGE, TILE), aligned(k, TILE + PAD)
            image_wide, moment_wide = vel[0, plane, around, :], moved[plane, m_around, :]
            image = image_wide[EDGE : EDGE + TILE]
            moment = moment_wide[EDGE : EDGE + TILE]
            row_wide = swapped[plane, a, 1, v_around, :]
            vel_c, vel_r = swapped[plane, a, 0, v_at, :], row_wide[EDGE : EDGE + TILE]
            vel_p = swapped[plane, a, 2, v_at, :]
            if keep_image is not None:
                over = jnp.where(plane == last, 0.0, vel[0, above, at, :])
                under = jnp.where(plane == 0, 0.0, vel[0, below, at, :])
                push = vel_c * along_cols(image) + vel_r * across(image_wide)
                keep_image(plane, k, image - scale * (push + vel_p * (over - under)))
            if keep_moment:
                over = moved[above, m_at, :] * swapped[above, a, 2, v_at, :]
                under = moved[below, m_at, :] * swapped[below, a, 2, v_at, :]
                over = jnp.where(plane == last, 0.0, over)
                under = jnp.where(plane == 0, 0.0, under)
                flux = along_cols(moment * vel_c) + across(moment_wide * row_wide) + (over - under)
                vel[1, plane, aligned(own + k, TILE), :] = moment - scale * flux

    def to_send(plane, k, value):
        vel[2, plane, aligned(mate_at + k, TILE), :] = value

    def to_keep(plane, k, value):
        image_in[plane, aligned(k, TILE), :] = value

    @pl.when(middle)
    def _():
        mix(1 - home_at)

        @pl.loop(0, planes)
        def _(plane):
            last_rows(plane, mate // 2, to_send, False)
            result(plane).start()

        mix(home_at)

        @pl.loop(0, planes)
        def _(plane):
            last_rows(plane, chip, to_keep, True)
            pull_turn(plane)

        @pl.loop(planes, planes + 2 * HOP)
        def _(turn):
            pull_turn(turn)

    @pl.when(is_end)
    def _():
        mix(home_at)

        @pl.loop(0, planes)
        def _(plane):
            last_rows(plane, chip, None, True)

        @pl.loop(planes + 3 - BEHIND, planes + 2 * HOP)
        def _(turn):
            pull_turn(turn)

    stores = [
        pltpu.make_async_copy(image_in, image_out.at[0], local_sems.at[1]),
        pltpu.make_async_copy(vel.at[1, :, moment_at, :], moment_out.at[0], local_sems.at[2]),
    ]
    for copy in stores:
        copy.start()

    stores.append(
        pltpu.make_async_copy(vel.at[1, :, new_at, :], template_out.at[0], local_sems.at[3])
    )
    stores[-1].start()
    block_planes = planes // 4
    mine = owned_block[grp]
    for k in range(block_planes):
        vel[2, k, owned_at, :] = vel[2, mine * block_planes + k, center_at, :]
    stores.append(
        pltpu.make_async_copy(
            vel.at[2, pl.ds(0, block_planes), owned_at, :], owned_out.at[0], local_sems.at[4]
        )
    )
    stores[-1].start()

    @pl.loop(0, planes)
    def _(plane):
        pull_copy(plane, 0).wait_send()
        pull_copy(plane, 1).wait_send()
        to_mate(plane, 0).wait_send()
        for which in range(chips):
            side(plane, which * 2 + core).wait_send()

        @pl.when(middle)
        def _():
            to_peer(plane, 0).wait_send()
            to_peer(plane, 1).wait_send()
            to_mate(plane, 1).wait_send()
            to_mate(plane, 2).wait_send()
            result(plane).wait_send()

    for copy in stores:
        copy.wait()


def on_device_whole(templates, momentum, subjects, smooth_x, smooth_y, smooth_z, owned_block):
    planes, own, cols = templates.shape[1:]
    rows = smooth_y.shape[0]
    chips = lax.axis_size("slab") // 2
    span, total = own + PAD, chips * (own + PAD)
    dims = (planes, rows, cols, own, chips)
    volume = jax.ShapeDtypeStruct(templates.shape, jnp.float32)
    owned = jax.ShapeDtypeStruct((1, planes // 4, own, cols), jnp.float32)
    any_space = pl.BlockSpec(memory_space=pl.ANY)
    smem = pl.BlockSpec(memory_space=pltpu.SMEM)
    f32 = lambda *shape: pltpu.VMEM(shape, jnp.float32)
    b16 = lambda *shape: pltpu.VMEM(shape, jnp.bfloat16)
    dma = lambda *shape: pltpu.SemaphoreType.DMA(shape)
    return pl.pallas_call(
        functools.partial(whole_kernel, dims),
        out_shape=(volume, volume, owned, volume),
        in_specs=[smem] * 2 + [any_space] * 5,
        out_specs=(any_space,) * 4,
        scratch_shapes=[
            f32(2, planes, rows + 2 * PAD, cols),
            f32(3, planes, total + PAD, cols),
            f32(planes, total, cols),
            b16(3, rows, cols),
            b16(3, rows, cols),
            f32(total, cols),
            f32(RING, 3, 4 * own + PAD, cols),
            f32(planes, 2, 3, span, cols),
            f32(planes, own, cols),
            f32(planes, own, cols),
            f32(planes, own, cols),
            f32(rows + PAD, cols),
            b16(total, rows),
            b16(total, rows),
            b16(cols, cols),
            b16(cols, cols),
            b16(4 * own + PAD, rows // 2),
            b16(4 * own + PAD, rows // 2),
            dma(5),
            dma(planes, 3),
            dma(planes, 2),
            dma(planes, chips),
            dma(planes, 2 * chips),
            dma(planes, 2),
            dma(planes, 2),
            dma(planes),
            dma(planes),
            dma(2, planes),
            dma(2, planes),
            dma(planes),
        ],
        compiler_params=pltpu.CompilerParams(
            collective_id=0, has_side_effects=True, vmem_limit_bytes=VMEM_LIMIT
        ),
        cost_estimate=pl.CostEstimate(
            flops=36 * planes * rows * rows * cols, bytes_accessed=2**24, transcendentals=0
        ),
    )(smooth_z, owned_block, templates, momentum, subjects, smooth_x, smooth_y)


def on_device(templates, momentum, subjects, smooth_x, smooth_y, smooth_z, owned_block):
    time_step = 1.0 / STEPS
    image = templates[0]
    moment = momentum[0]
    for section in range(STEPS):
        image_rows = with_halo(image, (("slab", 1),), 1)
        grad_rows = (image_rows[:, 2:, :] - image_rows[:, :-2, :]) * 0.5
        grad_cols = diff_cols(image)
        grad_planes = diff_planes(image)
        pushing = smooth_planes(
            jnp.stack([moment * grad_cols, moment * grad_rows, moment * grad_planes]), smooth_z
        )
        plane_fields = lax.all_to_all(pushing, "slab", split_axis=1, concat_axis=2, tiled=True)
        plane_vel = -smooth_plane(plane_fields, smooth_x, smooth_y)
        velocity = lax.all_to_all(plane_vel, "slab", split_axis=2, concat_axis=1, tiled=True)
        flux_edge = with_halo(moment * velocity[1], (("slab", 1),), 1)
        flux_rows = (flux_edge[:, 2:, :] - flux_edge[:, :-2, :]) * 0.5
        new_image = image - time_step * (
            velocity[0] * grad_cols + velocity[1] * grad_rows + velocity[2] * grad_planes
        )
        new_moment = moment - time_step * (
            diff_cols(moment * velocity[0]) + flux_rows + diff_planes(moment * velocity[2])
        )
        image = new_image
        moment = new_moment
    return finish(image, moment, templates, subjects, owned_block)


def finish(image, moment, templates, subjects, owned_block):
    update = templates[0] - learn_rate * (image - subjects[0])
    return (image[None], moment[None]) + pull(update, owned_block)


def sum_groups(field, orders):
    groups = lax.axis_size("grp")
    share = field.shape[0] // len(orders)
    pieces = [field[at * share : (at + 1) * share] for at in range(len(orders))]
    for turn in range(len(orders[0])):
        sent = [
            lax.ppermute(piece, "grp", [(i, i ^ order[turn]) for i in range(groups)])
            for piece, order in zip(pieces, orders)
        ]
        pieces = [piece + got for piece, got in zip(pieces, sent)]
    return jnp.concatenate(pieces, axis=0)


def pull(update, owned_block):
    groups = lax.axis_size("grp")
    planes_all = update.shape[0]
    block_planes = planes_all // groups
    if groups == 4 and planes_all % 2 == 0:
        center = sum_groups(update, ((1, 2), (2, 1))) / groups
    else:
        center = lax.psum(update, "grp") / groups
    owned_index = owned_block[lax.axis_index("grp")]
    owned_out = lax.dynamic_slice_in_dim(center, owned_index * block_planes, block_planes, 0)[None]
    new_template = update + pull_weight * (center - update)
    return (owned_out, new_template[None])


def solution(mesh):
    def body(*args):
        templates, smooth_y = args[0], args[4]
        gathered = 2 * 4 * templates.shape[1] * templates.shape[3] * smooth_y.shape[0]
        fits = gathered <= GATHER_BYTES and mesh.shape["grp"] == 4 and mesh.shape["slab"] == 8
        return (on_device_whole if fits else on_device)(*args)

    return jax.shard_map(
        body,
        mesh=mesh,
        in_specs=(
            P("grp", None, "slab", None),
            P("grp", None, "slab", None),
            P("grp", None, "slab", None),
            P(),
            P(),
            P(),
            P(),
        ),
        out_specs=(
            P("grp", None, "slab", None),
            P("grp", None, "slab", None),
            P("grp", None, "slab", None),
            P("grp", None, "slab", None),
        ),
        check_vma=False,
    )
```

```python
import functools

import jax
import jax.numpy as jnp
from jax import lax
from jax.experimental import pallas as pl
from jax.experimental.pallas import tpu as pltpu
from jax.sharding import PartitionSpec as P

STEPS = 2
GATHER_BYTES = 16 * 2**20
EDGE = 8
PAD = 2 * EDGE
TILE = 16
RING = 3
AHEAD = 3
LAG = 3
BEHIND = 2
HOP = 2
VMEM_LIMIT = 62 * 2**20
MESH_ID = pl.DeviceIdType.MESH


learn_rate = 0.5
pull_weight = 0.5


def with_halo(cells, sides, width):
    for axis, dim in sides:
        count = lax.axis_size(axis)
        ends = count - 1
        head = lax.slice_in_dim(cells, 0, width, axis=dim)
        tail = lax.slice_in_dim(cells, cells.shape[dim] - width, cells.shape[dim], axis=dim)
        cells = jnp.concatenate(
            [
                lax.ppermute(tail, axis, [(i, (i + 1) % count) for i in range(ends)]),
                cells,
                lax.ppermute(head, axis, [((i + 1) % count, i) for i in range(ends)]),
            ],
            axis=dim,
        )
    return cells


def diff_cols(field):
    zeros = jnp.zeros_like(field[..., :1])
    padded = jnp.concatenate([zeros, field, zeros], axis=-1)
    return (padded[..., 2:] - padded[..., :-2]) * 0.5


def diff_planes(field):
    zeros = jnp.zeros_like(field[..., :1, :, :])
    padded = jnp.concatenate([zeros, field, zeros], axis=-3)
    return (padded[..., 2:, :, :] - padded[..., :-2, :, :]) * 0.5


def smooth_planes(field, smooth_z):
    return jnp.einsum("ij,cjyx->ciyx", smooth_z, field, precision=lax.Precision.HIGHEST)


def smooth_plane(field, smooth_x, smooth_y):
    along = jnp.einsum("ij,cpyj->cpyi", smooth_x, field, precision=lax.Precision.HIGHEST)
    return jnp.einsum("ij,cpjx->cpix", smooth_y, along, precision=lax.Precision.HIGHEST)


def diff_rows(field):
    zeros = jnp.zeros_like(field[..., :1, :])
    padded = jnp.concatenate([zeros, field, zeros], axis=-2)
    return (padded[..., 2:, :] - padded[..., :-2, :]) * 0.5


def rows_of(field, start, count):
    return lax.dynamic_slice_in_dim(field, start, count, field.ndim - 2)


def halve(field):
    high = field.astype(jnp.bfloat16)
    return high, (field - high.astype(jnp.float32)).astype(jnp.bfloat16)


def dot_pair(left, right):
    mul = lambda a, b: jnp.dot(a, b, preferred_element_type=jnp.float32)
    return mul(left[0], right[0]) + (mul(left[0], right[1]) + mul(left[1], right[0]))


def aligned(start, size, step=8):
    return pl.ds(pl.multiple_of(start, step), size)


def across(wide):
    return wide[EDGE + 1 : EDGE + 1 + TILE] - wide[EDGE - 1 : EDGE - 1 + TILE]


def whole_kernel(
    dims, smooth_z, owned_block, templates, momentum, subjects, smooth_x, smooth_y,
    image_out, moment_out, owned_out, template_out,
    raw, vel, moved, high, low, along, parts, swapped, first_in, second_in, image_in,
    padded_y, ext_high, ext_low, cols_high, cols_low, win_high, win_low,
    local_sems, mate_sems, peer_sems, side_sems, recv_sems,
    part_send, part_recv, result_send, result_recv, pull_send, pull_recv, subject_sems,
):
    planes, rows, cols, own, chips = dims
    span = own + PAD
    pair = 2 * own
    half = rows // 2
    wide = 2 * pair + PAD
    me = lax.axis_index("slab")
    grp = lax.axis_index("grp")
    chip, core = me // 2, me % 2
    other = 1 - core
    sibling = chip * 2 + other
    middle = (chip == 1) | (chip == 2)
    is_end = (chip == 0) | (chip == 3)
    mate = jnp.where(chip % 2 == 0, me + 2, me - 2)
    peer = jnp.where(chip == 1, me + 2, jnp.where(chip == 2, me - 2, mate))
    peer_mate = jnp.where(chip == 1, me + 4, me - 4)
    scale = 0.5 / STEPS

    def own_rows(buffer_kind):
        return raw.at[buffer_kind, :, aligned(PAD + me * own, own), :]

    loads = [
        pltpu.make_async_copy(templates.at[0], own_rows(0), local_sems.at[0]),
        pltpu.make_async_copy(momentum.at[0], own_rows(1), local_sems.at[1]),
    ]
    mats = [
        pltpu.make_async_copy(smooth_y, padded_y.at[pl.ds(EDGE, rows), :], local_sems.at[2]),
        pltpu.make_async_copy(
            smooth_x.at[pl.ds(0, half), :], moved.at[0, pl.ds(0, half), :], local_sems.at[3]
        ),
        pltpu.make_async_copy(
            smooth_x.at[pl.ds(half, half), :], moved.at[1, pl.ds(0, half), :], local_sems.at[4]
        ),
    ]
    for copy in loads + mats:
        copy.start()

    barrier = pltpu.get_barrier_semaphore()

    def greet(where):
        pl.semaphore_signal(barrier, inc=1, device_id=where, device_id_type=MESH_ID)

    across_x = jnp.where(grp % 2 == 0, grp + 1, grp - 1)
    across_y = (grp + 2) % 4
    greet({"slab": mate})
    greet({"slab": sibling})
    greet({"grp": across_x})
    greet({"grp": across_y})

    @pl.when(middle)
    def _():
        greet({"slab": peer})

    pl.semaphore_wait(barrier, jnp.where(middle, 5, 4))

    for copy in loads:
        copy.wait()

    def send(plane, source, sem, target):
        piece = raw.at[:, plane, aligned(PAD + source * own, own), :]
        return pltpu.make_async_remote_copy(
            src_ref=piece, dst_ref=piece, send_sem=sem, recv_sem=recv_sems.at[plane, source],
            device_id={"slab": target}, device_id_type=MESH_ID,
        )

    def to_mate(plane, which):
        return send(plane, (me, peer, peer_mate)[which], mate_sems.at[plane, which], mate)

    def to_peer(plane, which):
        return send(plane, (me, mate)[which], peer_sems.at[plane, which], peer)

    def side(plane, source):
        return send(plane, source, side_sems.at[plane, source // 2], sibling)

    def arrived(plane, source):
        send(plane, source, side_sems.at[plane, 0], sibling).wait_recv()

    def send_own(plane):
        to_peer(plane, 0).start()
        side(plane, me).start()

    early = planes - 2

    ahead = min(AHEAD, planes)
    last = planes - 1
    lines = chips * span + PAD
    total = chips * span
    zeros_pad = jnp.zeros((PAD, cols), jnp.float32)
    column = lax.broadcasted_iota(jnp.int32, (TILE, cols), 1)
    is_first, is_last = column == 0, column == cols - 1

    def along_cols(tile):
        after = jnp.where(is_last, 0.0, pltpu.roll(tile, cols - 1, 1))
        return after - jnp.where(is_first, 0.0, pltpu.roll(tile, 1, 1))

    moment_at, update_at = pl.ds(own, own), pl.ds(2 * own, own)
    sum_at, new_at = pl.ds(3 * own, own), pl.ds(4 * own, own)
    center_at, owned_at = pl.ds(0, own), pl.ds(2 * own, own)
    mate_at = 3 * own

    def subject_load(plane):
        return pltpu.make_async_copy(
            subjects.at[0, plane], vel.at[1, plane, new_at, :], subject_sems.at[plane]
        )

    def result(plane):
        return pltpu.make_async_remote_copy(
            src_ref=vel.at[2, plane, pl.ds(mate_at, own), :], dst_ref=image_in.at[plane],
            send_sem=result_send.at[plane], recv_sem=result_recv.at[plane],
            device_id={"slab": mate}, device_id_type=MESH_ID,
        )

    def pull_copy(plane, phase):
        source = vel.at[1, plane, update_at if phase == 0 else sum_at, :]
        by_x = plane % 2 == phase
        return pltpu.make_async_remote_copy(
            src_ref=source, dst_ref=(first_in, second_in)[phase].at[plane],
            send_sem=pull_send.at[phase, plane], recv_sem=pull_recv.at[phase, plane],
            device_id={"grp": jnp.where(by_x, across_x, across_y)}, device_id_type=MESH_ID,
        )

    def pull_turn(turn):
        @pl.when(turn < planes)
        def _():
            plane = turn
            subject_load(plane).wait()

            @pl.when(is_end)
            def _():
                result(plane).wait_recv()

            template = raw[0, plane, aligned(PAD + me * own, own), :]
            subject = vel[1, plane, new_at, :]
            vel[1, plane, update_at, :] = template - learn_rate * (image_in[plane] - subject)
            pull_copy(plane, 0).start()

        @pl.when((turn >= HOP) & (turn < planes + HOP))
        def _():
            plane = turn - HOP
            pull_copy(plane, 0).wait_recv()
            vel[1, plane, sum_at, :] = vel[1, plane, update_at, :] + first_in[plane]
            pull_copy(plane, 1).start()

        @pl.when((turn >= 2 * HOP) & (turn < planes + 2 * HOP))
        def _():
            plane = turn - 2 * HOP
            pull_copy(plane, 1).wait_recv()
            center = (vel[1, plane, sum_at, :] + second_in[plane]) * 0.25
            update = vel[1, plane, update_at, :]
            vel[2, plane, center_at, :] = center
            vel[1, plane, new_at, :] = update + pull_weight * (center - update)

    @pl.when(is_end)
    def _():
        for plane in range(planes):
            to_mate(plane, 0).start()
        for plane in range(planes):
            side(plane, me).start()

    @pl.when(middle)
    def _():
        for plane in range(ahead):
            send_own(plane)
        for plane in range(2):
            to_mate(plane, 0).start()

    from_mate = (mate, mate + (mate - me), mate + 2 * (mate - me))

    for kind in range(2):
        for plane in range(planes):
            raw[kind, plane, pl.ds(0, PAD), :] = zeros_pad
            raw[kind, plane, pl.ds(PAD + rows, PAD), :] = zeros_pad
    zeros_edge = jnp.zeros((EDGE, cols), jnp.float32)
    padded_y[pl.ds(0, EDGE), :] = zeros_edge
    padded_y[pl.ds(EDGE + rows, EDGE), :] = zeros_edge

    @pl.loop(0, 3 * planes)
    def _(at):
        @pl.loop(0, lines // TILE, unroll=3)
        def _(t):
            vel[at // planes, at % planes, aligned(t * TILE, TILE), :] = zeros_pad

    for copy in mats:
        copy.wait()
    turned = jnp.concatenate(
        [moved[0, pl.ds(0, half), :].T, moved[1, pl.ds(0, half), :].T], axis=1
    )
    cols_high[...], cols_low[...] = halve(turned)
    for b in range(chips):
        piece = padded_y[aligned(b * pair + core * own, span), :]
        ext_high[pl.ds(b * span, span), :], ext_low[pl.ds(b * span, span), :] = halve(piece)
    window = padded_y[aligned((chip // 2) * 2 * pair, wide), :]
    window = jnp.concatenate(
        [
            jnp.where(core == 0, window[:, b * pair : b * pair + own],
                      window[:, b * pair + own : (b + 1) * pair])
            for b in range(chips)
        ],
        axis=1,
    )
    win_high[...], win_low[...] = halve(window)

    def keep(where, field, value):
        top = value.astype(jnp.bfloat16)
        high[field, where, :] = top
        low[field, where, :] = (value - top.astype(jnp.float32)).astype(jnp.bfloat16)

    def smooth(field, weights):
        along[...] = dot_pair((ext_high[...], ext_low[...]), (high[field], low[field]))
        along[...] = dot_pair(halve(along[...]), (cols_high[...], cols_low[...]))

        @pl.loop(0, total // TILE, unroll=4)
        def _(t):
            tile = along[aligned(t * TILE, TILE), :]
            into = aligned(EDGE + t * TILE, TILE)
            for i in range(planes):
                vel[field, i, into, :] += weights[i] * tile

    def plane_weights(plane):
        return [-0.5 * smooth_z[i, plane] for i in range(planes)]

    def pass_on(plane):
        @pl.when(plane + ahead < planes)
        def _():
            send_own(plane + ahead)

        @pl.when(plane < early // 2 - 1)
        def _():
            to_mate(2 * plane + 2, 0).start()
            to_mate(2 * plane + 3, 0).start()

        @pl.when(plane >= early)
        def _():
            to_mate(plane, 0).start()

        arrived(plane, mate)
        to_peer(plane, 1).start()
        side(plane, mate).start()

    def smooth_plane_fields(plane):
        @pl.when(middle)
        def _():
            for which, source in ((1, peer), (2, peer_mate)):
                arrived(plane, source)
                to_mate(plane, which).start()
                side(plane, source).start()

        @pl.when(is_end)
        def _():
            for source in from_mate:
                arrived(plane, source)
                side(plane, source).start()

        for which in range(chips):
            arrived(plane, which * 2 + other)

        before = jnp.maximum(plane - 1, 0)
        far = jnp.maximum(plane - 2, 0)

        @pl.loop(0, rows // TILE, unroll=8)
        def _(t):
            here = aligned(PAD + t * TILE, TILE)
            into = aligned(t * TILE, TILE, TILE)
            wide_tile = raw[0, plane, aligned(EDGE + t * TILE, TILE + PAD), :]
            image, moment = wide_tile[EDGE : EDGE + TILE], raw[1, plane, here, :]
            keep(into, 0, moment * along_cols(image))
            keep(into, 1, moment * across(wide_tile))
            under = jnp.where(plane >= 2, raw[0, far, here, :], 0.0)
            keep(into, 2, raw[1, before, here, :] * (image - under))

        @pl.loop(0, total // TILE, unroll=10)
        def _(t):
            b, k = t // (span // TILE), t % (span // TILE)
            here = aligned(b * pair + core * own + k * TILE + EDGE, TILE)
            moved[plane, aligned(t * TILE, TILE), :] = along_cols(raw[0, plane, here, :])

        smooth(0, plane_weights(plane))
        smooth(1, plane_weights(plane))
        smooth(2, [jnp.where(plane >= 1, w, 0.0) for w in plane_weights(before)])

    lag = jnp.where(middle, LAG, 0)

    @pl.loop(0, planes + LAG)
    def _(turn):
        @pl.when(middle & (turn < planes))
        def _():
            pass_on(turn)

        @pl.when((turn >= lag) & (turn < planes + lag))
        def _():
            smooth_plane_fields(turn - lag)

    @pl.loop(0, rows // TILE, unroll=8)
    def _(t):
        here = aligned(PAD + t * TILE, TILE)
        keep(aligned(t * TILE, TILE, TILE), 2, raw[1, last, here, :] * (0.0 - raw[0, last - 1, here, :]))

    smooth(2, plane_weights(last))

    def part_copy(plane, a):
        return pltpu.make_async_remote_copy(
            src_ref=parts.at[plane % RING, :, aligned(a * pair + other * own, span), :],
            dst_ref=swapped.at[plane, a],
            send_sem=part_send.at[plane, a], recv_sem=part_recv.at[plane, a],
            device_id={"slab": sibling}, device_id_type=MESH_ID,
        )

    needed = [middle | (chip % 2 == a) for a in range(2)]
    home_at = chip % 2

    @pl.loop(0, planes + 3)
    def _(turn):
        @pl.when(turn < planes)
        def _():
            plane = turn
            above, below = jnp.minimum(plane + 1, last), jnp.maximum(plane - 1, 0)

            @pl.loop(0, total // TILE, unroll=10)
            def _(t):
                b, k = t // (span // TILE), t % (span // TILE)
                g = b * pair + core * own + k * TILE + EDGE
                here, around = aligned(g, TILE), aligned(g - EDGE, TILE + PAD)
                at, at_around = aligned(t * TILE + EDGE, TILE), aligned(t * TILE, TILE + PAD)
                image_wide, moment_wide = raw[0, plane, around, :], raw[1, plane, around, :]
                image = image_wide[EDGE : EDGE + TILE]
                moment = moment_wide[EDGE : EDGE + TILE]
                row_wide = vel[1, plane, at_around, :]
                vel_c, vel_r = vel[0, plane, at, :], row_wide[EDGE : EDGE + TILE]
                vel_p = vel[2, plane, at, :]
                over = jnp.where(plane == last, 0.0, raw[0, above, here, :])
                under = jnp.where(plane == 0, 0.0, raw[0, below, here, :])
                push = (
                    vel_c * moved[plane, aligned(t * TILE, TILE), :]
                    + vel_r * across(image_wide) + vel_p * (over - under)
                )
                over = jnp.where(plane == last, 0.0, raw[1, above, here, :] * vel[2, above, at, :])
                under = jnp.where(plane == 0, 0.0, raw[1, below, here, :] * vel[2, below, at, :])
                flux = (
                    along_cols(moment * vel_c) + across(moment_wide * row_wide) + (over - under)
                )
                vel[0, plane, at, :] = image - scale * push
                moved[plane, aligned(t * TILE, TILE), :] = moment - scale * flux

        @pl.when((turn >= 1) & (turn <= planes))
        def _():
            plane = turn - 1
            above, below = jnp.minimum(plane + 1, last), jnp.maximum(plane - 1, 0)

            @pl.loop(0, half // TILE, unroll=16)
            def _(t):
                b, k = t // (own // TILE), t % (own // TILE)
                e = b * span + k * TILE + PAD
                at = aligned(e, TILE)
                into = aligned(t * TILE, TILE, TILE)
                image_wide = vel[0, plane, aligned(e - EDGE, TILE + PAD), :]
                image = image_wide[EDGE : EDGE + TILE]
                moment = moved[plane, aligned(e - EDGE, TILE), :]
                over = jnp.where(plane == last, 0.0, vel[0, above, at, :])
                under = jnp.where(plane == 0, 0.0, vel[0, below, at, :])
                keep(into, 0, moment * along_cols(image))
                keep(into, 1, moment * across(image_wide))
                keep(into, 2, moment * (over - under))

            @pl.when(plane >= RING)
            def _():
                for a in range(2):
                    @pl.when(needed[a])
                    def _(a=a):
                        part_copy(plane - RING, a).wait_send()

            inner = pl.ds(0, half)

            @pl.when(middle)
            def _():
                for field in range(3):
                    parts[plane % RING, field] = dot_pair(
                        (win_high[...], win_low[...]),
                        (high[field, inner, :], low[field, inner, :]),
                    )

            @pl.when(is_end)
            def _():
                lines_at = aligned(home_at * pair, pair + PAD, TILE)
                for field in range(3):
                    parts[plane % RING, field, lines_at, :] = dot_pair(
                        (win_high[lines_at, :], win_low[lines_at, :]),
                        (high[field, inner, :], low[field, inner, :]),
                    )

            for a in range(2):
                @pl.when(needed[a])
                def _(a=a):
                    part_copy(plane, a).start()

            subject_load(plane).start()

        @pl.when(turn >= 3)
        def _():
            plane = turn - 3
            for a in range(2):
                @pl.when(needed[a])
                def _(a=a):
                    part_copy(plane, a).wait_recv()
                    mine = parts[plane % RING, :, aligned(a * pair + core * own, span), :]
                    both = (mine + swapped[plane, a]).reshape(3 * span, cols)
                    out = dot_pair(halve(both), (cols_high[...], cols_low[...]))
                    swapped[plane, a] = out.reshape(3, span, cols)

        @pl.when(is_end & (turn >= BEHIND))
        def _():
            pull_turn(turn - BEHIND)

    for plane in range(max(planes - RING, 0), planes):
        for a in range(2):
            @pl.when(needed[a])
            def _(a=a):
                part_copy(plane, a).wait_send()

    def mix(a):
        @pl.loop(0, 3 * (span // 8), unroll=2)
        def _(t):
            field, where = t // (span // 8), aligned((t % (span // 8)) * 8, 8)
            held = [swapped[j, a, field, where, :] for j in range(planes)]
            for i in range(planes):
                swapped[i, a, field, where, :] = -0.5 * sum(
                    smooth_z[i, j] * held[j] for j in range(planes)
                )

    def last_rows(plane, home, keep_image, keep_moment):
        above, below = jnp.minimum(plane + 1, last), jnp.maximum(plane - 1, 0)
        a = home % 2

        @pl.loop(0, own // TILE, unroll=4)
        def _(t):
            k = t * TILE
            e = home * span + k + PAD
            at, around = aligned(e, TILE), aligned(e - EDGE, TILE + PAD)
            m_at, m_around = aligned(e - EDGE, TILE), aligned(e - PAD, TILE + PAD)
            v_at, v_around = aligned(k + EDGE, TILE), aligned(k, TILE + PAD)
            image_wide, moment_wide = vel[0, plane, around, :], moved[plane, m_around, :]
            image = image_wide[EDGE : EDGE + TILE]
            moment = moment_wide[EDGE : EDGE + TILE]
            row_wide = swapped[plane, a, 1, v_around, :]
            vel_c, vel_r = swapped[plane, a, 0, v_at, :], row_wide[EDGE : EDGE + TILE]
            vel_p = swapped[plane, a, 2, v_at, :]
            if keep_image is not None:
                over = jnp.where(plane == last, 0.0, vel[0, above, at, :])
                under = jnp.where(plane == 0, 0.0, vel[0, below, at, :])
                push = vel_c * along_cols(image) + vel_r * across(image_wide)
                keep_image(plane, k, image - scale * (push + vel_p * (over - under)))
            if keep_moment:
                over = moved[above, m_at, :] * swapped[above, a, 2, v_at, :]
                under = moved[below, m_at, :] * swapped[below, a, 2, v_at, :]
                over = jnp.where(plane == last, 0.0, over)
                under = jnp.where(plane == 0, 0.0, under)
                flux = along_cols(moment * vel_c) + across(moment_wide * row_wide) + (over - under)
                vel[1, plane, aligned(own + k, TILE), :] = moment - scale * flux

    def to_send(plane, k, value):
        vel[2, plane, aligned(mate_at + k, TILE), :] = value

    def to_keep(plane, k, value):
        image_in[plane, aligned(k, TILE), :] = value

    @pl.when(middle)
    def _():
        mix(1 - home_at)

        @pl.loop(0, planes)
        def _(plane):
            last_rows(plane, mate // 2, to_send, False)
            result(plane).start()

        mix(home_at)

        @pl.loop(0, planes)
        def _(plane):
            last_rows(plane, chip, to_keep, True)
            pull_turn(plane)

        @pl.loop(planes, planes + 2 * HOP)
        def _(turn):
            pull_turn(turn)

    @pl.when(is_end)
    def _():
        mix(home_at)

        @pl.loop(0, planes)
        def _(plane):
            last_rows(plane, chip, None, True)

        @pl.loop(planes + 3 - BEHIND, planes + 2 * HOP)
        def _(turn):
            pull_turn(turn)

    stores = [
        pltpu.make_async_copy(image_in, image_out.at[0], local_sems.at[1]),
        pltpu.make_async_copy(vel.at[1, :, moment_at, :], moment_out.at[0], local_sems.at[2]),
    ]
    for copy in stores:
        copy.start()

    stores.append(
        pltpu.make_async_copy(vel.at[1, :, new_at, :], template_out.at[0], local_sems.at[3])
    )
    stores[-1].start()
    block_planes = planes // 4
    mine = owned_block[grp]
    for k in range(block_planes):
        vel[2, k, owned_at, :] = vel[2, mine * block_planes + k, center_at, :]
    stores.append(
        pltpu.make_async_copy(
            vel.at[2, pl.ds(0, block_planes), owned_at, :], owned_out.at[0], local_sems.at[4]
        )
    )
    stores[-1].start()

    @pl.loop(0, planes)
    def _(plane):
        pull_copy(plane, 0).wait_send()
        pull_copy(plane, 1).wait_send()
        to_mate(plane, 0).wait_send()
        for which in range(chips):
            side(plane, which * 2 + core).wait_send()

        @pl.when(middle)
        def _():
            to_peer(plane, 0).wait_send()
            to_peer(plane, 1).wait_send()
            to_mate(plane, 1).wait_send()
            to_mate(plane, 2).wait_send()
            result(plane).wait_send()

    for copy in stores:
        copy.wait()


def on_device_whole(templates, momentum, subjects, smooth_x, smooth_y, smooth_z, owned_block):
    planes, own, cols = templates.shape[1:]
    rows = smooth_y.shape[0]
    chips = lax.axis_size("slab") // 2
    span, total = own + PAD, chips * (own + PAD)
    dims = (planes, rows, cols, own, chips)
    volume = jax.ShapeDtypeStruct(templates.shape, jnp.float32)
    owned = jax.ShapeDtypeStruct((1, planes // 4, own, cols), jnp.float32)
    any_space = pl.BlockSpec(memory_space=pl.ANY)
    smem = pl.BlockSpec(memory_space=pltpu.SMEM)
    f32 = lambda *shape: pltpu.VMEM(shape, jnp.float32)
    b16 = lambda *shape: pltpu.VMEM(shape, jnp.bfloat16)
    dma = lambda *shape: pltpu.SemaphoreType.DMA(shape)
    return pl.pallas_call(
        functools.partial(whole_kernel, dims),
        out_shape=(volume, volume, owned, volume),
        in_specs=[smem] * 2 + [any_space] * 5,
        out_specs=(any_space,) * 4,
        scratch_shapes=[
            f32(2, planes, rows + 2 * PAD, cols),
            f32(3, planes, total + PAD, cols),
            f32(planes, total, cols),
            b16(3, rows, cols),
            b16(3, rows, cols),
            f32(total, cols),
            f32(RING, 3, 4 * own + PAD, cols),
            f32(planes, 2, 3, span, cols),
            f32(planes, own, cols),
            f32(planes, own, cols),
            f32(planes, own, cols),
            f32(rows + PAD, cols),
            b16(total, rows),
            b16(total, rows),
            b16(cols, cols),
            b16(cols, cols),
            b16(4 * own + PAD, rows // 2),
            b16(4 * own + PAD, rows // 2),
            dma(5),
            dma(planes, 3),
            dma(planes, 2),
            dma(planes, chips),
            dma(planes, 2 * chips),
            dma(planes, 2),
            dma(planes, 2),
            dma(planes),
            dma(planes),
            dma(2, planes),
            dma(2, planes),
            dma(planes),
        ],
        compiler_params=pltpu.CompilerParams(
            collective_id=0, has_side_effects=True, vmem_limit_bytes=VMEM_LIMIT
        ),
        cost_estimate=pl.CostEstimate(
            flops=36 * planes * rows * rows * cols, bytes_accessed=2**24, transcendentals=0
        ),
    )(smooth_z, owned_block, templates, momentum, subjects, smooth_x, smooth_y)


def on_device(templates, momentum, subjects, smooth_x, smooth_y, smooth_z, owned_block):
    time_step = 1.0 / STEPS
    image = templates[0]
    moment = momentum[0]
    for section in range(STEPS):
        image_rows = with_halo(image, (("slab", 1),), 1)
        grad_rows = (image_rows[:, 2:, :] - image_rows[:, :-2, :]) * 0.5
        grad_cols = diff_cols(image)
        grad_planes = diff_planes(image)
        pushing = smooth_planes(
            jnp.stack([moment * grad_cols, moment * grad_rows, moment * grad_planes]), smooth_z
        )
        plane_fields = lax.all_to_all(pushing, "slab", split_axis=1, concat_axis=2, tiled=True)
        plane_vel = -smooth_plane(plane_fields, smooth_x, smooth_y)
        velocity = lax.all_to_all(plane_vel, "slab", split_axis=2, concat_axis=1, tiled=True)
        flux_edge = with_halo(moment * velocity[1], (("slab", 1),), 1)
        flux_rows = (flux_edge[:, 2:, :] - flux_edge[:, :-2, :]) * 0.5
        new_image = image - time_step * (
            velocity[0] * grad_cols + velocity[1] * grad_rows + velocity[2] * grad_planes
        )
        new_moment = moment - time_step * (
            diff_cols(moment * velocity[0]) + flux_rows + diff_planes(moment * velocity[2])
        )
        image = new_image
        moment = new_moment
    return finish(image, moment, templates, subjects, owned_block)


def finish(image, moment, templates, subjects, owned_block):
    update = templates[0] - learn_rate * (image - subjects[0])
    return (image[None], moment[None]) + pull(update, owned_block)


def sum_groups(field, orders):
    groups = lax.axis_size("grp")
    share = field.shape[0] // len(orders)
    pieces = [field[at * share : (at + 1) * share] for at in range(len(orders))]
    for turn in range(len(orders[0])):
        sent = [
            lax.ppermute(piece, "grp", [(i, i ^ order[turn]) for i in range(groups)])
            for piece, order in zip(pieces, orders)
        ]
        pieces = [piece + got for piece, got in zip(pieces, sent)]
    return jnp.concatenate(pieces, axis=0)


def pull(update, owned_block):
    groups = lax.axis_size("grp")
    planes_all = update.shape[0]
    block_planes = planes_all // groups
    if groups == 4 and planes_all % 2 == 0:
        center = sum_groups(update, ((1, 2), (2, 1))) / groups
    else:
        center = lax.psum(update, "grp") / groups
    owned_index = owned_block[lax.axis_index("grp")]
    owned_out = lax.dynamic_slice_in_dim(center, owned_index * block_planes, block_planes, 0)[None]
    new_template = update + pull_weight * (center - update)
    return (owned_out, new_template[None])


def solution(mesh):
    def body(*args):
        templates, smooth_y = args[0], args[4]
        gathered = 2 * 4 * templates.shape[1] * templates.shape[3] * smooth_y.shape[0]
        fits = gathered <= GATHER_BYTES and mesh.shape["grp"] == 4 and mesh.shape["slab"] == 8
        return (on_device_whole if fits else on_device)(*args)

    return jax.shard_map(
        body,
        mesh=mesh,
        in_specs=(
            P("grp", None, "slab", None),
            P("grp", None, "slab", None),
            P("grp", None, "slab", None),
            P(),
            P(),
            P(),
            P(),
        ),
        out_specs=(
            P("grp", None, "slab", None),
            P("grp", None, "slab", None),
            P("grp", None, "slab", None),
            P("grp", None, "slab", None),
        ),
        check_vma=False,
    )
```
